512 devices in a mesh: dp: 32 (over x_lo, z), seq: 4 (over y), mp: 4 (over x_hi, core).
Axes of the slice: x: 4 (x_hi: 2, x_lo: 2; x = x_hi * 2 + x_lo), y: 4, z: 16, core: 2. Of those that a mesh axis runs over, the one named last changes fastest.
Arguments:
- hidden: bfloat16 [32768, 6656], P(('dp', 'seq'), 'mp'), may hold values from -6 to 6
- cotangent: bfloat16 [32768, 17920], P(('dp', 'seq'), 'mp'), may hold values from -6 to 6
- frozen_down: bfloat16 [6656, 4], P('mp'), may hold values from -0.078125 to 0.078125
- adapter: float32 [4, 4, 4480], P('mp', None, ('dp', 'seq')), may hold values from -6 to 6
- prior: float32 [48], replicated, may hold values from 0.2 to 5
- domain_of: int32 [64], P('dp'), may hold values from 0 to 47
Outputs:
- new_adapter: float32 [4, 4, 4480], P('mp', None, ('dp', 'seq'))
- log_weights: float32 [48], replicated
The draws below stay inside these ranges and needn't reach their ends.
All inputs are finite; a program needn't handle non-finite values.
Results may differ from the reference program's by a relative error of at most 0.014.
Values may be sent and summed in bfloat16 or wider, within the bound.
A program may use at most 64 MiB of HBM per device.

```python
import math
import jax
import jax.numpy as jnp
from jax import lax

D = 6656
FF = 17920
NDOM = 48
RANK = 4
SEQS = 2
PIECE = 128
ROWS = 256
TOKENS = 32768
SEQUENCES = 64
FFM = 4480
N_DP = 32
N_SEQ = 4
N_MP = 4


def plant(array, rng, least, largest):
    place = [jax.random.randint(jax.random.fold_in(rng, axis), (), 0, length) for axis, length in enumerate(array.shape)]
    widest = array.shape.index(max(array.shape))
    neighbour = place[:widest] + [(place[widest] + 1) % array.shape[widest]] + place[widest + 1:]
    return array.at[tuple(place)].set(least).at[tuple(neighbour)].set(largest)


def block_levels(own_key, extent, cuts, least, top_value):
    factor_of, own = 1.0, jax.random.fold_in(own_key, 6)
    for position, parts in cuts:
        steps = jnp.exp(jax.random.uniform(jax.random.fold_in(own, position), (parts,), jnp.float32, least / len(cuts), top_value / len(cuts)))
        factor_of = factor_of * jnp.repeat(steps, extent[position] // parts).reshape([-1 if axis == position else 1 for axis in range(len(extent))])
    return factor_of


def bell_draw(own_key, dims, deviation, bound, split=(), kind=jnp.bfloat16):
    drawn = deviation * jax.random.normal(own_key, dims, jnp.float32)
    if split:
        drawn = drawn * block_levels(own_key, dims, split, -0.22, 0.18)
    return jnp.clip(drawn, -bound, bound).astype(kind)


def setup_inputs(seed: int = 0) -> dict:
    seeds = jax.random.split(jax.random.key(seed), 7)
    hidden = bell_draw(seeds[0], (TOKENS, D), 1.0, 6.0, ((0, 128), (1, 4)))
    cotangent = bell_draw(seeds[1], (TOKENS, FF), 1.0, 6.0, ((0, 128), (1, 4)))
    frozen_down = bell_draw(seeds[2], (D, RANK), D ** -0.5, 0.078125, ((0, 4),))
    adapter = bell_draw(seeds[3], (N_MP, RANK, FFM), 1.0, 6.0, ((0, 4), (2, 128)), jnp.float32)
    prior = jnp.clip(jnp.exp(jax.random.uniform(seeds[4], (NDOM,), jnp.float32, math.log(0.2), math.log(5.0))), 0.2, 5.0)
    domain_of = plant(jax.random.randint(seeds[5], (SEQUENCES,), 0, NDOM), jax.random.fold_in(seeds[5], 1), 0, NDOM - 1).astype(jnp.int32)
    return {"hidden": hidden, "cotangent": cotangent, "frozen_down": frozen_down, "adapter": adapter, "prior": prior, "domain_of": domain_of}


step_rate = 1.0
learn_rate = 0.5

def reference(hidden, cotangent, frozen_down, adapter, prior, domain_of):
    block_width = D // N_MP
    down = jnp.zeros((TOKENS, RANK), jnp.float32)
    for block in range(N_MP):
        part_prod = jnp.dot(hidden[:, block * block_width:(block + 1) * block_width], frozen_down[block * block_width:(block + 1) * block_width, :], preferred_element_type=jnp.float32)
        down = down + part_prod.astype(jnp.bfloat16).astype(jnp.float32)
    coef = down.astype(jnp.bfloat16).astype(jnp.float32)
    domain_tok = jnp.broadcast_to(domain_of.reshape(N_DP, 1, SEQS, 1), (N_DP, N_SEQ, SEQS, PIECE)).reshape(TOKENS)
    onehot = (domain_tok[:, None] == jnp.arange(NDOM, dtype=jnp.int32)[None, :]).astype(jnp.float32)
    spread = (onehot[:, :, None] * coef[:, None, :]).reshape(TOKENS, NDOM * RANK)
    group_rows = N_SEQ * ROWS

    def accumulate(total, index):
        block = lax.dynamic_slice_in_dim(spread, index * group_rows, group_rows, 0)
        cols = lax.dynamic_slice_in_dim(cotangent, index * group_rows, group_rows, 0).astype(jnp.float32)
        return (total + jnp.dot(block.T, cols, preferred_element_type=jnp.float32), None)
    total, unused = lax.scan(accumulate, jnp.zeros((NDOM * RANK, FF), jnp.float32), jnp.arange(N_DP, dtype=jnp.int32))
    grads = total.reshape(NDOM, RANK, FF)
    weights = prior / jnp.sum(prior)
    mixture = jnp.einsum('i,irf->rf', weights, grads, precision=lax.Precision.HIGHEST)
    sumsq = jnp.sum(mixture * mixture)
    scores = jnp.einsum('irf,rf->i', grads, mixture, precision=lax.Precision.HIGHEST)
    meansq = sumsq / (RANK * FF) + 1e-06
    ratio = scores / (RANK * FF * meansq)
    raised = weights * jnp.exp(step_rate * ratio)
    log_new = jnp.log(weights) + step_rate * ratio - jnp.log(jnp.sum(raised))
    new_w = jnp.exp(log_new)
    update = jnp.einsum('i,irf->rf', new_w, grads, precision=lax.Precision.HIGHEST)
    full = adapter.transpose(1, 0, 2).reshape(RANK, FF)
    moved = full - learn_rate * update / jnp.sqrt(meansq)
    new_adapter = moved.reshape(RANK, N_MP, FFM).transpose(1, 0, 2)
    return (new_adapter, log_new)
```

```python
import functools

import jax
import jax.numpy as jnp
from jax import lax
from jax.experimental import pallas as pl
from jax.experimental.pallas import tpu as pltpu
from jax.sharding import PartitionSpec as P

FF = 17920
NDOM = 48
RANK = 4
ROWS = 256
PIECE = 128
DM = 1664
FFM = 4480
N_DP = 32
N_SEQ = 4
N_MP = 4
COLS = FFM // (N_DP * N_SEQ)
LANES = 128
HALF = 64
CHUNKS = 7
WIDTH = FFM // CHUNKS

SEND = jnp.bfloat16
MESH = pl.DeviceIdType.MESH
step_rate = 1.0
learn_rate = 0.5


def kernel(
    hid_hbm, cot_hbm, fro_hbm, ada_hbm, pri_hbm, dom_hbm,
    out_ref, log_ref,
    hid, cot, fro, ada, pri, dom, wrow, part, lhs, g, spread, seqbuf, total, got, gotf, rows_a, rows_b,
    in_sem, cot_sem, small_sem, s1, r1, s2, r2, s3, r3, s4, r4, s5, r5,
):
    dp, seq, mp = lax.axis_index("dp"), lax.axis_index("seq"), lax.axis_index("mp")

    def to(d=0, s=0, m=0):
        return {
            "dp": lax.rem(dp + d, N_DP),
            "seq": lax.rem(seq + s, N_SEQ),
            "mp": lax.rem(mp + m, N_MP),
        }

    def send(src, dst, ssem, rsem, **where):
        copy = pltpu.make_async_remote_copy(
            src_ref=src, dst_ref=dst, send_sem=ssem, recv_sem=rsem,
            device_id=to(**where), device_id_type=MESH,
        )
        copy.start()

    def done(ref, ssem, rsem, **where):
        return pltpu.make_async_remote_copy(
            src_ref=ref, dst_ref=ref, send_sem=ssem, recv_sem=rsem,
            device_id=to(**where), device_id_type=MESH,
        )

    barrier = pltpu.get_barrier_semaphore()
    plane = [(s, m) for s in range(N_SEQ) for m in range(N_MP) if (s, m) != (0, 0)]
    for s, m in plane:
        pl.semaphore_signal(barrier, inc=1, device_id=to(s=s, m=m), device_id_type=MESH)
    for j in range(1, N_DP):
        pl.semaphore_signal(barrier, inc=1, device_id=to(d=j), device_id_type=MESH)

    loads = [
        pltpu.make_async_copy(fro_hbm, fro, in_sem.at[0]),
        pltpu.make_async_copy(hid_hbm, hid, in_sem.at[1]),
    ]
    for load in loads:
        load.start()
    cot_loads = []
    for c in range(CHUNKS):
        cut = pl.ds(c * WIDTH, WIDTH)
        load = pltpu.make_async_copy(cot_hbm.at[:, cut], cot.at[:, cut], cot_sem.at[c])
        load.start()
        cot_loads.append(load)
    small = [
        pltpu.make_async_copy(ada_hbm, ada, small_sem.at[0]),
        pltpu.make_async_copy(pri_hbm, pri, small_sem.at[1]),
        pltpu.make_async_copy(dom_hbm, dom, small_sem.at[2]),
    ]
    for load in small:
        load.start()

    lhs[...] = jnp.zeros_like(lhs)
    wrow[...] = jnp.zeros_like(wrow)

    for load in loads:
        load.wait()
    partial = lax.dot_general(
        fro[...], hid[...], (((1,), (1,)), ((), ())), preferred_element_type=jnp.float32
    )
    part[0] = partial.astype(jnp.bfloat16).astype(jnp.float32)

    pl.semaphore_wait(barrier, len(plane) + N_DP - 1)

    for m in range(1, N_MP):
        send(part.at[0], part.at[m], s1, r1, m=m)
    done(part.at[pl.ds(1, N_MP - 1)], s1, r1, m=1).wait_recv()
    down = part[0] + part[1] + part[2] + part[3]
    token = lax.broadcasted_iota(jnp.int32, (RANK, ROWS), 1)
    lhs[0:RANK] = jnp.where(token < PIECE, down, 0.0)
    lhs[8 : 8 + RANK] = jnp.where(token < PIECE, 0.0, down)
    left = lhs[...].astype(jnp.bfloat16)
    for c in range(CHUNKS):
        cut = slice(c * WIDTH, (c + 1) * WIDTH)
        cot_loads[c].wait()
        g[:, cut] = jnp.dot(left, cot[:, cut], preferred_element_type=jnp.float32)

    lane = lax.broadcasted_iota(jnp.int32, (8, LANES), 1)
    for p in range(N_DP * N_SEQ):
        v, o = divmod(p * COLS, LANES)
        a = g[0:8, v * LANES : (v + 1) * LANES]
        b = g[8:16, v * LANES : (v + 1) * LANES]
        a = a if o == 0 else pltpu.roll(a, LANES - o, 1)
        b = pltpu.roll(b, (HALF - o) % LANES, 1) if o != HALF else b
        if o + COLS > LANES:
            a2 = g[0:8, (v + 1) * LANES : (v + 2) * LANES]
            b2 = g[8:16, (v + 1) * LANES : (v + 2) * LANES]
            a2 = pltpu.roll(a2, LANES - o, 1)
            b2 = pltpu.roll(b2, (HALF - o) % LANES, 1) if o != HALF else b2
            a = jnp.where(lane < LANES - o, a, a2)
            b = jnp.where(lane < HALF + LANES - o, b, b2)
        joined = jnp.where(lane < HALF, a, b)
        spread[p % N_SEQ, p // N_SEQ] = joined[0:RANK].astype(SEND)

    for s in range(1, N_SEQ):
        send(spread.at[lax.rem(seq + s, N_SEQ)], seqbuf.at[s - 1], s2, r2, s=s)
    for load in small:
        load.wait()
    d0 = dom[0].astype(jnp.float32)
    d1 = dom[1].astype(jnp.float32)
    done(seqbuf, s2, r2, s=1).wait_recv()
    f32 = jnp.float32
    summed = (
        spread[seq].astype(f32) + seqbuf[0].astype(f32) + seqbuf[1].astype(f32) + seqbuf[2].astype(f32)
    )
    lane3 = lax.broadcasted_iota(jnp.int32, (N_DP, RANK, LANES), 2)
    summed = jnp.where(lane3 == COLS, d0, jnp.where(lane3 == HALF + COLS, d1, summed))
    total[...] = summed.astype(SEND)

    for j in range(1, N_DP):
        send(total.at[lax.rem(dp + j, N_DP)], got.at[j], s3, r3, d=j)
    got[0] = total[dp]

    wrow[:, 0:NDOM] = pri[...]
    prior = wrow[...]
    weights = prior / jnp.sum(prior, axis=1, keepdims=True)
    lane1 = lax.broadcasted_iota(jnp.int32, (1, LANES), 1)
    lane2 = lax.broadcasted_iota(jnp.int32, (N_DP, LANES), 1)
    low = lane2 < HALF

    done(got.at[pl.ds(1, N_DP - 1)], s3, r3, d=1).wait_recv()
    gotf[...] = got[...].astype(f32)
    rank_rows = [gotf[:, r, :] for r in range(RANK)]
    dom0 = jnp.sum(jnp.where(lane2 == COLS, rank_rows[0], 0.0), axis=1, keepdims=True)
    dom1 = jnp.sum(jnp.where(lane2 == HALF + COLS, rank_rows[0], 0.0), axis=1, keepdims=True)
    lanef = lane2.astype(f32)
    hot0 = (lanef == dom0).astype(f32)
    hot1 = (lanef == dom1).astype(f32)

    def per_sequence(row):
        return jnp.where(
            low,
            jnp.sum(hot0 * row, axis=1, keepdims=True),
            jnp.sum(hot1 * row, axis=1, keepdims=True),
        )

    def combine(scale):
        sums = [jnp.sum(scale * x, axis=0, keepdims=True) for x in rank_rows]
        return [x + pltpu.roll(x, HALF, 1) for x in sums]

    valid = (lane1 < COLS) | ((lane1 >= HALF) & (lane1 < HALF + COLS))
    mixture = [jnp.where(valid, x, 0.0) for x in combine(per_sequence(weights))]
    square = sum(x * x for x in mixture)
    sumsq = jnp.sum(jnp.where(lane1 < HALF, square, 0.0), axis=1, keepdims=True)
    product = sum(x * y for x, y in zip(rank_rows, mixture))
    score0 = jnp.sum(jnp.where(low, product, 0.0), axis=1, keepdims=True)
    score1 = jnp.sum(jnp.where(low, 0.0, product), axis=1, keepdims=True)
    row = jnp.sum(hot0 * score0 + hot1 * score1, axis=0, keepdims=True)
    row = jnp.where(lane1 == LANES - 1, sumsq, row)

    mine = seq * N_MP + mp
    rows_a[mine] = row
    for s, m in plane:
        send(rows_a.at[mine], rows_a.at[mine], s4, r4, s=s, m=m)
    done(rows_a.at[pl.ds(0, len(plane))], s4, r4, s=1).wait_recv()
    row = jnp.sum(rows_a[...], axis=0)
    rows_b[dp] = row
    for j in range(1, N_DP):
        send(rows_b.at[dp], rows_b.at[dp], s5, r5, d=j)
    done(rows_b.at[pl.ds(0, N_DP - 1)], s5, r5, d=1).wait_recv()
    row = jnp.sum(rows_b[...], axis=0)

    sumsq = jnp.sum(jnp.where(lane1 == LANES - 1, row, 0.0), axis=1, keepdims=True)
    scores = jnp.where(lane1 < NDOM, row, 0.0)
    meansq = sumsq / (RANK * FF) + 1e-06
    ratio = scores / (RANK * FF * meansq)
    raised = weights * jnp.exp(step_rate * ratio)
    log_new = jnp.log(weights) + step_rate * ratio - jnp.log(jnp.sum(raised, axis=1, keepdims=True))
    log_ref[...] = log_new[:, 0:NDOM]
    new = jnp.where(lane1 < NDOM, jnp.exp(log_new), 0.0)
    update = combine(per_sequence(new))
    root = jnp.sqrt(meansq)
    for r in range(RANK):
        moved = learn_rate * update[r] / root
        out_ref[r : r + 1, :] = ada[r : r + 1, :] - moved[:, 0:COLS]

    done(part.at[pl.ds(1, N_MP - 1)], s1, r1, m=1).wait_send()
    done(seqbuf, s2, r2, s=1).wait_send()
    done(got.at[pl.ds(1, N_DP - 1)], s3, r3, d=1).wait_send()
    done(rows_a.at[pl.ds(0, len(plane))], s4, r4, s=1).wait_send()
    done(rows_b.at[pl.ds(0, N_DP - 1)], s5, r5, d=1).wait_send()


def body(hidden, cotangent, frozen_down, adapter, prior, domain_of):
    f32 = jnp.float32
    sem = pltpu.SemaphoreType.DMA
    out, log_new = pl.pallas_call(
        kernel,
        out_shape=(
            jax.ShapeDtypeStruct((RANK, COLS), f32),
            jax.ShapeDtypeStruct((1, NDOM), f32),
        ),
        in_specs=[pl.BlockSpec(memory_space=pl.ANY)] * 6,
        out_specs=(pl.BlockSpec(memory_space=pltpu.VMEM),) * 2,
        scratch_shapes=[
            pltpu.VMEM((ROWS, DM), jnp.bfloat16),
            pltpu.VMEM((ROWS, FFM), jnp.bfloat16),
            pltpu.VMEM((RANK, DM), jnp.bfloat16),
            pltpu.VMEM((RANK, COLS), f32),
            pltpu.VMEM((1, NDOM), f32),
            pltpu.SMEM((2,), jnp.int32),
            pltpu.VMEM((1, LANES), f32),
            pltpu.VMEM((N_MP, RANK, ROWS), f32),
            pltpu.VMEM((16, ROWS), f32),
            pltpu.VMEM((16, FFM), f32),
            pltpu.VMEM((N_SEQ, N_DP, RANK, LANES), SEND),
            pltpu.VMEM((N_SEQ - 1, N_DP, RANK, LANES), SEND),
            pltpu.VMEM((N_DP, RANK, LANES), SEND),
            pltpu.VMEM((N_DP, RANK, LANES), SEND),
            pltpu.VMEM((N_DP, RANK, LANES), f32),
            pltpu.VMEM((N_SEQ * N_MP, 1, LANES), f32),
            pltpu.VMEM((N_DP, 1, LANES), f32),
            sem((2,)),
            sem((CHUNKS,)),
            sem((3,)),
        ]
        + [sem] * 10,
        compiler_params=pltpu.CompilerParams(
            collective_id=0, has_side_effects=True, vmem_limit_bytes=60 << 20
        ),
    )(hidden, cotangent, frozen_down.T, adapter.reshape(RANK, COLS), prior.reshape(1, NDOM), domain_of)
    return out.reshape(1, RANK, COLS), log_new.reshape(NDOM)


def solution(mesh):
    return jax.shard_map(
        body,
        mesh=mesh,
        in_specs=(
            P(("dp", "seq"), "mp"),
            P(("dp", "seq"), "mp"),
            P("mp", None),
            P("mp", None, ("dp", "seq")),
            P(),
            P("dp"),
        ),
        out_specs=(P("mp", None, ("dp", "seq")), P()),
        check_vma=False,
    )
```

```python
import functools

import jax
import jax.numpy as jnp
from jax import lax
from jax.experimental import pallas as pl
from jax.experimental.pallas import tpu as pltpu
from jax.sharding import PartitionSpec as P

FF = 17920
NDOM = 48
RANK = 4
ROWS = 256
PIECE = 128
DM = 1664
FFM = 4480
N_DP = 32
N_SEQ = 4
N_MP = 4
COLS = FFM // (N_DP * N_SEQ)
LANES = 128
HALF = 64
CHUNKS = 7
WIDTH = FFM // CHUNKS

SEND = jnp.bfloat16
N_Z = 16
ORDER = (0, 1, 2, 3, 4, 5, 6, 7, 15, 8, 14, 9, 13, 10, 12, 11)
MESH = pl.DeviceIdType.MESH
step_rate = 1.0
learn_rate = 0.5


def kernel(
    hid_hbm, cot_hbm, fro_hbm, ada_hbm, pri_hbm, dom_hbm,
    out_ref, log_ref,
    hid, cot, fro, ada, pri, dom, wrow, part, lhs, g, spread, seqbuf, total, got, gotf, rows_a, rows_b,
    in_sem, cot_sem, small_sem, s1, r1, s2, r2, s3, r3, s4, r4, s5, r5, ready,
):
    dp, seq, mp = lax.axis_index("dp"), lax.axis_index("seq"), lax.axis_index("mp")

    def to(d=0, s=0, m=0):
        return {
            "dp": lax.rem(dp + d, N_DP),
            "seq": lax.rem(seq + s, N_SEQ),
            "mp": lax.rem(mp + m, N_MP),
        }

    z = lax.rem(dp, N_Z)
    place = jnp.where(z < 8, z, jnp.where(z < 12, 2 * z - 7, 38 - 2 * z))

    def at(d):
        return {"dp": d, "seq": seq, "mp": mp}

    def send(src, dst, ssem, rsem, target=None, **where):
        copy = pltpu.make_async_remote_copy(
            src_ref=src, dst_ref=dst, send_sem=ssem, recv_sem=rsem,
            device_id=to(**where) if target is None else target, device_id_type=MESH,
        )
        copy.start()

    def done(ref, ssem, rsem, **where):
        return pltpu.make_async_remote_copy(
            src_ref=ref, dst_ref=ref, send_sem=ssem, recv_sem=rsem,
            device_id=to(**where), device_id_type=MESH,
        )

    barrier = pltpu.get_barrier_semaphore()
    plane = [(s, m) for s in range(N_SEQ) for m in range(N_MP) if (s, m) != (0, 0)]
    for s, m in plane:
        pl.semaphore_signal(barrier, inc=1, device_id=to(s=s, m=m), device_id_type=MESH)
    pl.semaphore_signal(barrier, inc=1, device_id=to(d=N_Z), device_id_type=MESH)
    for position, plane_z in enumerate(ORDER):

        @pl.when(place < position)
        def _():
            for x in range(2):
                pl.semaphore_signal(barrier, inc=1, device_id=at(x * N_Z + plane_z), device_id_type=MESH)


    loads = [
        pltpu.make_async_copy(fro_hbm, fro, in_sem.at[0]),
        pltpu.make_async_copy(hid_hbm, hid, in_sem.at[1]),
    ]
    for load in loads:
        load.start()
    cot_loads = []
    for c in range(CHUNKS):
        cut = pl.ds(c * WIDTH, WIDTH)
        load = pltpu.make_async_copy(cot_hbm.at[:, cut], cot.at[:, cut], cot_sem.at[c])
        load.start()
        cot_loads.append(load)
    small = [
        pltpu.make_async_copy(ada_hbm, ada, small_sem.at[0]),
        pltpu.make_async_copy(pri_hbm, pri, small_sem.at[1]),
        pltpu.make_async_copy(dom_hbm, dom, small_sem.at[2]),
    ]
    for load in small:
        load.start()

    lhs[...] = jnp.zeros_like(lhs)
    wrow[...] = jnp.zeros_like(wrow)

    for load in loads:
        load.wait()
    partial = lax.dot_general(
        fro[...], hid[...], (((1,), (1,)), ((), ())), preferred_element_type=jnp.float32
    )
    part[0] = partial.astype(jnp.bfloat16).astype(jnp.float32)

    pl.semaphore_wait(barrier, len(plane) + 1 + 2 * place)
    for position, plane_z in enumerate(ORDER):

        @pl.when(place > position)
        def _():
            for x in range(2):
                pl.semaphore_signal(
                    ready.at[z], inc=1, device_id=at(x * N_Z + plane_z), device_id_type=MESH
                )

    for m in range(1, N_MP):
        send(part.at[0], part.at[m], s1, r1, m=m)
    done(part.at[pl.ds(1, N_MP - 1)], s1, r1, m=1).wait_recv()
    down = part[0] + part[1] + part[2] + part[3]
    token = lax.broadcasted_iota(jnp.int32, (RANK, ROWS), 1)
    lhs[0:RANK] = jnp.where(token < PIECE, down, 0.0)
    lhs[8 : 8 + RANK] = jnp.where(token < PIECE, 0.0, down)
    left = lhs[...].astype(jnp.bfloat16)
    for c in range(CHUNKS):
        cut = slice(c * WIDTH, (c + 1) * WIDTH)
        cot_loads[c].wait()
        g[:, cut] = jnp.dot(left, cot[:, cut], preferred_element_type=jnp.float32)

    lane = lax.broadcasted_iota(jnp.int32, (8, LANES), 1)
    for p in range(N_DP * N_SEQ):
        v, o = divmod(p * COLS, LANES)
        a = g[0:8, v * LANES : (v + 1) * LANES]
        b = g[8:16, v * LANES : (v + 1) * LANES]
        a = a if o == 0 else pltpu.roll(a, LANES - o, 1)
        b = pltpu.roll(b, (HALF - o) % LANES, 1) if o != HALF else b
        if o + COLS > LANES:
            a2 = g[0:8, (v + 1) * LANES : (v + 2) * LANES]
            b2 = g[8:16, (v + 1) * LANES : (v + 2) * LANES]
            a2 = pltpu.roll(a2, LANES - o, 1)
            b2 = pltpu.roll(b2, (HALF - o) % LANES, 1) if o != HALF else b2
            a = jnp.where(lane < LANES - o, a, a2)
            b = jnp.where(lane < HALF + LANES - o, b, b2)
        joined = jnp.where(lane < HALF, a, b)
        spread[p % N_SEQ, p // N_SEQ] = joined[0:RANK].astype(SEND)

    for s in range(1, N_SEQ):
        send(spread.at[lax.rem(seq + s, N_SEQ)], seqbuf.at[s - 1], s2, r2, s=s)
    for load in small:
        load.wait()
    d0 = dom[0].astype(jnp.float32)
    d1 = dom[1].astype(jnp.float32)
    done(seqbuf, s2, r2, s=1).wait_recv()
    f32 = jnp.float32
    summed = (
        spread[seq].astype(f32) + seqbuf[0].astype(f32) + seqbuf[1].astype(f32) + seqbuf[2].astype(f32)
    )
    lane3 = lax.broadcasted_iota(jnp.int32, (N_DP, RANK, LANES), 2)
    summed = jnp.where(lane3 == COLS, d0, jnp.where(lane3 == HALF + COLS, d1, summed))
    total[...] = summed.astype(SEND)

    partner = lax.rem(dp + N_Z, N_DP)
    send(total.at[partner], got.at[dp], s3, r3, target=at(partner))
    for position, plane_z in enumerate(ORDER):

        @pl.when(place < position)
        def _():
            pl.semaphore_wait(ready.at[plane_z], 2)

        @pl.when(place != position)
        def _():
            for x in range(2):
                d = x * N_Z + plane_z
                send(total.at[d], got.at[dp], s3, r3, target=at(d))

    got[dp] = total[dp]

    wrow[:, 0:NDOM] = pri[...]
    prior = wrow[...]
    weights = prior / jnp.sum(prior, axis=1, keepdims=True)
    lane1 = lax.broadcasted_iota(jnp.int32, (1, LANES), 1)
    lane2 = lax.broadcasted_iota(jnp.int32, (N_DP, LANES), 1)
    low = lane2 < HALF

    done(got.at[pl.ds(0, N_DP - 1)], s3, r3, d=1).wait_recv()
    gotf[...] = got[...].astype(f32)
    rank_rows = [gotf[:, r, :] for r in range(RANK)]
    dom0 = jnp.sum(jnp.where(lane2 == COLS, rank_rows[0], 0.0), axis=1, keepdims=True)
    dom1 = jnp.sum(jnp.where(lane2 == HALF + COLS, rank_rows[0], 0.0), axis=1, keepdims=True)
    lanef = lane2.astype(f32)
    hot0 = (lanef == dom0).astype(f32)
    hot1 = (lanef == dom1).astype(f32)

    def per_sequence(row):
        return jnp.where(
            low,
            jnp.sum(hot0 * row, axis=1, keepdims=True),
            jnp.sum(hot1 * row, axis=1, keepdims=True),
        )

    def combine(scale):
        sums = [jnp.sum(scale * x, axis=0, keepdims=True) for x in rank_rows]
        return [x + pltpu.roll(x, HALF, 1) for x in sums]

    valid = (lane1 < COLS) | ((lane1 >= HALF) & (lane1 < HALF + COLS))
    mixture = [jnp.where(valid, x, 0.0) for x in combine(per_sequence(weights))]
    square = sum(x * x for x in mixture)
    sumsq = jnp.sum(jnp.where(lane1 < HALF, square, 0.0), axis=1, keepdims=True)
    product = sum(x * y for x, y in zip(rank_rows, mixture))
    score0 = jnp.sum(jnp.where(low, product, 0.0), axis=1, keepdims=True)
    score1 = jnp.sum(jnp.where(low, 0.0, product), axis=1, keepdims=True)
    row = jnp.sum(hot0 * score0 + hot1 * score1, axis=0, keepdims=True)
    row = jnp.where(lane1 == LANES - 1, sumsq, row)

    mine = seq * N_MP + mp
    rows_a[mine] = row
    for s, m in plane:
        send(rows_a.at[mine], rows_a.at[mine], s4, r4, s=s, m=m)
    done(rows_a.at[pl.ds(0, len(plane))], s4, r4, s=1).wait_recv()
    row = jnp.sum(rows_a[...], axis=0)
    rows_b[dp] = row
    for j in range(1, N_DP):
        send(rows_b.at[dp], rows_b.at[dp], s5, r5, d=j)
    done(rows_b.at[pl.ds(0, N_DP - 1)], s5, r5, d=1).wait_recv()
    row = jnp.sum(rows_b[...], axis=0)

    sumsq = jnp.sum(jnp.where(lane1 == LANES - 1, row, 0.0), axis=1, keepdims=True)
    scores = jnp.where(lane1 < NDOM, row, 0.0)
    meansq = sumsq / (RANK * FF) + 1e-06
    ratio = scores / (RANK * FF * meansq)
    raised = weights * jnp.exp(step_rate * ratio)
    log_new = jnp.log(weights) + step_rate * ratio - jnp.log(jnp.sum(raised, axis=1, keepdims=True))
    log_ref[...] = log_new[:, 0:NDOM]
    new = jnp.where(lane1 < NDOM, jnp.exp(log_new), 0.0)
    update = combine(per_sequence(new))
    root = jnp.sqrt(meansq)
    for r in range(RANK):
        moved = learn_rate * update[r] / root
        out_ref[r : r + 1, :] = ada[r : r + 1, :] - moved[:, 0:COLS]

    done(part.at[pl.ds(1, N_MP - 1)], s1, r1, m=1).wait_send()
    done(seqbuf, s2, r2, s=1).wait_send()
    done(got.at[pl.ds(0, N_DP - 1)], s3, r3, d=1).wait_send()
    done(rows_a.at[pl.ds(0, len(plane))], s4, r4, s=1).wait_send()
    done(rows_b.at[pl.ds(0, N_DP - 1)], s5, r5, d=1).wait_send()


def tail(moved, log_new, out_ref, log_ref):
    out_ref[...] = moved[...]
    log_ref[...] = log_new[...]


def body(hidden, cotangent, frozen_down, adapter, prior, domain_of):
    f32 = jnp.float32
    sem = pltpu.SemaphoreType.DMA
    out, log_new = pl.pallas_call(
        kernel,
        out_shape=(
            jax.ShapeDtypeStruct((RANK, COLS), f32),
            jax.ShapeDtypeStruct((1, NDOM), f32),
        ),
        in_specs=[pl.BlockSpec(memory_space=pl.ANY)] * 6,
        out_specs=(pl.BlockSpec(memory_space=pltpu.VMEM),) * 2,
        scratch_shapes=[
            pltpu.VMEM((ROWS, DM), jnp.bfloat16),
            pltpu.VMEM((ROWS, FFM), jnp.bfloat16),
            pltpu.VMEM((RANK, DM), jnp.bfloat16),
            pltpu.VMEM((RANK, COLS), f32),
            pltpu.VMEM((1, NDOM), f32),
            pltpu.SMEM((2,), jnp.int32),
            pltpu.VMEM((1, LANES), f32),
            pltpu.VMEM((N_MP, RANK, ROWS), f32),
            pltpu.VMEM((16, ROWS), f32),
            pltpu.VMEM((16, FFM), f32),
            pltpu.VMEM((N_SEQ, N_DP, RANK, LANES), SEND),
            pltpu.VMEM((N_SEQ - 1, N_DP, RANK, LANES), SEND),
            pltpu.VMEM((N_DP, RANK, LANES), SEND),
            pltpu.VMEM((N_DP, RANK, LANES), SEND),
            pltpu.VMEM((N_DP, RANK, LANES), f32),
            pltpu.VMEM((N_SEQ * N_MP, 1, LANES), f32),
            pltpu.VMEM((N_DP, 1, LANES), f32),
            sem((2,)),
            sem((CHUNKS,)),
            sem((3,)),
        ]
        + [sem] * 10
        + [pltpu.SemaphoreType.REGULAR((N_Z,))],
        compiler_params=pltpu.CompilerParams(
            collective_id=0, has_side_effects=True, vmem_limit_bytes=60 << 20
        ),
    )(hidden, cotangent, frozen_down.T, adapter.reshape(RANK, COLS), prior.reshape(1, NDOM), domain_of)
    out, log_new = pl.pallas_call(
        tail,
        out_shape=(
            jax.ShapeDtypeStruct((RANK, COLS), f32),
            jax.ShapeDtypeStruct((1, NDOM), f32),
        ),
        in_specs=[pl.BlockSpec(memory_space=pltpu.VMEM)] * 2,
        out_specs=(pl.BlockSpec(memory_space=pltpu.VMEM),) * 2,
    )(out, log_new)
    return out.reshape(1, RANK, COLS), log_new.reshape(NDOM)


def solution(mesh):
    return jax.shard_map(
        body,
        mesh=mesh,
        in_specs=(
            P(("dp", "seq"), "mp"),
            P(("dp", "seq"), "mp"),
            P("mp", None),
            P("mp", None, ("dp", "seq")),
            P(),
            P("dp"),
        ),
        out_specs=(P("mp", None, ("dp", "seq")), P()),
        check_vma=False,
    )
```

```python
import functools

import jax
import jax.numpy as jnp
from jax import lax
from jax.experimental import pallas as pl
from jax.experimental.pallas import tpu as pltpu
from jax.sharding import PartitionSpec as P

FF = 17920
NDOM = 48
RANK = 4
ROWS = 256
PIECE = 128
DM = 1664
FFM = 4480
N_DP = 32
N_SEQ = 4
N_MP = 4
COLS = FFM // (N_DP * N_SEQ)
LANES = 128
HALF = 64
CHUNKS = 2
SPAN = N_DP // CHUNKS
EDGES = tuple(min(c * 2304, FFM) for c in range(CHUNKS + 1))

SEND = jnp.bfloat16
N_Z = 16
ORDER = (0, 1, 2, 3, 4, 5, 6, 7, 15, 8, 14, 9, 13, 10, 12, 11)
MESH = pl.DeviceIdType.MESH
step_rate = 1.0
learn_rate = 0.5


def kernel(
    hid_hbm, cot_hbm, fro_hbm, ada_hbm, pri_hbm, dom_hbm,
    out_ref, log_ref,
    hid, cot, fro, ada, pri, dom, wrow, part, lhs, g, spread, seqbuf, total, got, gotf, rows_a, rows_b,
    in_sem, cot_sem, small_sem, s1, r1, s2, r2, s3, r3, s4, r4, s5, r5, ready,
):
    dp, seq, mp = lax.axis_index("dp"), lax.axis_index("seq"), lax.axis_index("mp")

    def to(d=0, s=0, m=0):
        return {
            "dp": lax.rem(dp + d, N_DP),
            "seq": lax.rem(seq + s, N_SEQ),
            "mp": lax.rem(mp + m, N_MP),
        }

    z = lax.rem(dp, N_Z)
    place = jnp.where(z < 8, z, jnp.where(z < 12, 2 * z - 7, 38 - 2 * z))

    def at(d):
        return {"dp": d, "seq": seq, "mp": mp}

    def send(src, dst, ssem, rsem, target=None, **where):
        copy = pltpu.make_async_remote_copy(
            src_ref=src, dst_ref=dst, send_sem=ssem, recv_sem=rsem,
            device_id=to(**where) if target is None else target, device_id_type=MESH,
        )
        copy.start()

    def done(ref, ssem, rsem, **where):
        return pltpu.make_async_remote_copy(
            src_ref=ref, dst_ref=ref, send_sem=ssem, recv_sem=rsem,
            device_id=to(**where), device_id_type=MESH,
        )

    loads = [
        pltpu.make_async_copy(fro_hbm, fro, in_sem.at[0]),
        pltpu.make_async_copy(hid_hbm, hid, in_sem.at[1]),
    ]
    for load in loads:
        load.start()
    barrier = pltpu.get_barrier_semaphore()
    plane = [(s, m) for s in (2, 1, 3, 0) for m in (2, 3, 1, 0) if (s, m) != (0, 0)]
    near = [(0, m) for m in range(1, N_MP)] + [(s, 0) for s in range(1, N_SEQ)]
    for s, m in near:
        pl.semaphore_signal(barrier, inc=1, device_id=to(s=s, m=m), device_id_type=MESH)
    pl.semaphore_signal(barrier, inc=1, device_id=to(d=N_Z), device_id_type=MESH)
    for position, plane_z in enumerate(ORDER):

        @pl.when(place < position)
        def _():
            for x in range(2):
                pl.semaphore_signal(barrier, inc=1, device_id=at(x * N_Z + plane_z), device_id_type=MESH)


    lhs[...] = jnp.zeros_like(lhs)
    wrow[...] = jnp.zeros_like(wrow)

    for load in loads:
        load.wait()
    cot_loads = []
    for c in range(CHUNKS):
        cut = pl.ds(EDGES[c], EDGES[c + 1] - EDGES[c])
        load = pltpu.make_async_copy(cot_hbm.at[:, cut], cot.at[:, cut], cot_sem.at[c])
        load.start()
        cot_loads.append(load)
    small = [
        pltpu.make_async_copy(ada_hbm, ada, small_sem.at[0]),
        pltpu.make_async_copy(pri_hbm, pri, small_sem.at[1]),
        pltpu.make_async_copy(dom_hbm, dom, small_sem.at[2]),
    ]
    for load in small:
        load.start()

    partial = lax.dot_general(
        fro[...], hid[...], (((1,), (1,)), ((), ())), preferred_element_type=jnp.float32
    )
    part[0] = partial.astype(jnp.bfloat16).astype(jnp.float32)

    pl.semaphore_wait(barrier, len(near) + 1 + 2 * place)
    for position, plane_z in enumerate(ORDER):

        @pl.when(place > position)
        def _():
            for x in range(2):
                pl.semaphore_signal(
                    ready.at[z], inc=1, device_id=at(x * N_Z + plane_z), device_id_type=MESH
                )

    for m in range(1, N_MP):
        send(part.at[0], part.at[m], s1, r1, m=m)
    done(part.at[pl.ds(1, N_MP - 1)], s1, r1, m=1).wait_recv()
    down = part[0] + part[1] + part[2] + part[3]
    token = lax.broadcasted_iota(jnp.int32, (RANK, ROWS), 1)
    lhs[0:RANK] = jnp.where(token < PIECE, down, 0.0)
    lhs[8 : 8 + RANK] = jnp.where(token < PIECE, 0.0, down)
    left = lhs[...].astype(jnp.bfloat16)
    lane = lax.broadcasted_iota(jnp.int32, (8, LANES), 1)
    for c in range(CHUNKS):
        cut = slice(EDGES[c], EDGES[c + 1])
        cot_loads[c].wait()
        g[:, cut] = jnp.dot(left, cot[:, cut], preferred_element_type=jnp.float32)
        for p in range(c * SPAN * N_SEQ, (c + 1) * SPAN * N_SEQ):
            v, o = divmod(p * COLS, LANES)
            a = g[0:8, v * LANES : (v + 1) * LANES]
            b = g[8:16, v * LANES : (v + 1) * LANES]
            a = a if o == 0 else pltpu.roll(a, LANES - o, 1)
            b = pltpu.roll(b, (HALF - o) % LANES, 1) if o != HALF else b
            if o + COLS > LANES:
                a2 = g[0:8, (v + 1) * LANES : (v + 2) * LANES]
                b2 = g[8:16, (v + 1) * LANES : (v + 2) * LANES]
                a2 = pltpu.roll(a2, LANES - o, 1)
                b2 = pltpu.roll(b2, (HALF - o) % LANES, 1) if o != HALF else b2
                a = jnp.where(lane < LANES - o, a, a2)
                b = jnp.where(lane < HALF + LANES - o, b, b2)
            joined = jnp.where(lane < HALF, a, b)
            spread[p % N_SEQ, p // N_SEQ] = joined[0:RANK].astype(SEND)
        part_of = pl.ds(c * SPAN, SPAN)
        for s in (2, 1, 3):
            send(spread.at[lax.rem(seq + s, N_SEQ), part_of], seqbuf.at[s - 1, part_of], s2, r2, s=s)

    for load in small:
        load.wait()
    d0 = dom[0].astype(jnp.float32)
    d1 = dom[1].astype(jnp.float32)
    done(seqbuf, s2, r2, s=1).wait_recv()
    f32 = jnp.float32
    summed = (
        spread[seq].astype(f32) + seqbuf[0].astype(f32) + seqbuf[1].astype(f32) + seqbuf[2].astype(f32)
    )
    lane3 = lax.broadcasted_iota(jnp.int32, (N_DP, RANK, LANES), 2)
    summed = jnp.where(lane3 == COLS, d0, jnp.where(lane3 == HALF + COLS, d1, summed))
    total[...] = summed.astype(SEND)

    partner = lax.rem(dp + N_Z, N_DP)
    send(total.at[partner], got.at[dp], s3, r3, target=at(partner))
    for position, plane_z in enumerate(ORDER):

        @pl.when(place < position)
        def _():
            pl.semaphore_wait(ready.at[plane_z], 2)

        @pl.when(place != position)
        def _():
            for x in range(2):
                d = x * N_Z + plane_z
                send(total.at[d], got.at[dp], s3, r3, target=at(d))

    got[dp] = total[dp]

    wrow[:, 0:NDOM] = pri[...]
    prior = wrow[...]
    weights = prior / jnp.sum(prior, axis=1, keepdims=True)
    lane1 = lax.broadcasted_iota(jnp.int32, (1, LANES), 1)
    lane2 = lax.broadcasted_iota(jnp.int32, (N_DP, LANES), 1)
    low = lane2 < HALF

    done(got.at[pl.ds(0, N_DP - 1)], s3, r3, d=1).wait_recv()
    gotf[...] = got[...].astype(f32)
    rank_rows = [gotf[:, r, :] for r in range(RANK)]
    dom0 = rank_rows[0][:, COLS : COLS + 1]
    dom1 = rank_rows[0][:, HALF + COLS : HALF + COLS + 1]
    lanef = lane2.astype(f32)
    hot0 = (lanef == dom0).astype(f32)
    hot1 = (lanef == dom1).astype(f32)

    def per_sequence(row):
        return jnp.where(
            low,
            jnp.sum(hot0 * row, axis=1, keepdims=True),
            jnp.sum(hot1 * row, axis=1, keepdims=True),
        )

    def combine(scale):
        sums = [jnp.sum(scale * x, axis=0, keepdims=True) for x in rank_rows]
        return [x + pltpu.roll(x, HALF, 1) for x in sums]

    valid = (lane1 < COLS) | ((lane1 >= HALF) & (lane1 < HALF + COLS))
    mixture = [jnp.where(valid, x, 0.0) for x in combine(per_sequence(weights))]
    square = sum(x * x for x in mixture)
    sumsq = jnp.sum(jnp.where(lane1 < HALF, square, 0.0), axis=1, keepdims=True)
    product = sum(x * y for x, y in zip(rank_rows, mixture))
    score0 = jnp.sum(jnp.where(low, product, 0.0), axis=1, keepdims=True)
    score1 = jnp.sum(jnp.where(low, 0.0, product), axis=1, keepdims=True)
    row = jnp.sum(hot0 * score0 + hot1 * score1, axis=0, keepdims=True)
    row = jnp.where(lane1 == LANES - 1, sumsq, row)

    mine = (dp // N_Z * N_SEQ + seq) * N_MP + mp
    rows_a[mine] = row
    slab = [(d, s, m) for s in (2, 1, 3, 0) for d in (N_Z, 0) for m in (2, 3, 1, 0)][:-1]
    for d, s, m in slab:
        send(rows_a.at[mine], rows_a.at[mine], s4, r4, d=d, s=s, m=m)
    done(rows_a.at[pl.ds(0, len(slab))], s4, r4, s=1).wait_recv()
    row = jnp.sum(rows_a[...], axis=0)
    rows_b[z] = row
    for j in (8, 7, 9, 6, 10, 5, 11, 4, 12, 3, 13, 2, 14, 1, 15):
        send(rows_b.at[z], rows_b.at[z], s5, r5, target=at(dp - z + lax.rem(z + j, N_Z)))
    done(rows_b.at[pl.ds(0, N_Z - 1)], s5, r5, d=1).wait_recv()
    row = jnp.sum(rows_b[...], axis=0)

    sumsq = jnp.sum(jnp.where(lane1 == LANES - 1, row, 0.0), axis=1, keepdims=True)
    scores = jnp.where(lane1 < NDOM, row, 0.0)
    meansq = sumsq / (RANK * FF) + 1e-06
    ratio = scores / (RANK * FF * meansq)
    raised = weights * jnp.exp(step_rate * ratio)
    log_new = jnp.log(weights) + step_rate * ratio - jnp.log(jnp.sum(raised, axis=1, keepdims=True))
    log_ref[...] = log_new[:, 0:NDOM]
    new = jnp.where(lane1 < NDOM, jnp.exp(log_new), 0.0)
    update = combine(per_sequence(new))
    root = jnp.sqrt(meansq)
    for r in range(RANK):
        moved = learn_rate * update[r] / root
        out_ref[r : r + 1, :] = ada[r : r + 1, :] - moved[:, 0:COLS]

    done(part.at[pl.ds(1, N_MP - 1)], s1, r1, m=1).wait_send()
    done(seqbuf, s2, r2, s=1).wait_send()
    done(got.at[pl.ds(0, N_DP - 1)], s3, r3, d=1).wait_send()
    done(rows_a.at[pl.ds(0, len(slab))], s4, r4, s=1).wait_send()
    done(rows_b.at[pl.ds(0, N_Z - 1)], s5, r5, d=1).wait_send()


def tail(moved, log_new, out_ref, log_ref):
    out_ref[...] = moved[...]
    log_ref[...] = log_new[...]


def body(hidden, cotangent, frozen_down, adapter, prior, domain_of):
    f32 = jnp.float32
    sem = pltpu.SemaphoreType.DMA
    out, log_new = pl.pallas_call(
        kernel,
        out_shape=(
            jax.ShapeDtypeStruct((RANK, COLS), f32),
            jax.ShapeDtypeStruct((1, NDOM), f32),
        ),
        in_specs=[pl.BlockSpec(memory_space=pl.ANY)] * 6,
        out_specs=(pl.BlockSpec(memory_space=pltpu.VMEM),) * 2,
        scratch_shapes=[
            pltpu.VMEM((ROWS, DM), jnp.bfloat16),
            pltpu.VMEM((ROWS, FFM), jnp.bfloat16),
            pltpu.VMEM((RANK, DM), jnp.bfloat16),
            pltpu.VMEM((RANK, COLS), f32),
            pltpu.VMEM((1, NDOM), f32),
            pltpu.SMEM((2,), jnp.int32),
            pltpu.VMEM((1, LANES), f32),
            pltpu.VMEM((N_MP, RANK, ROWS), f32),
            pltpu.VMEM((16, ROWS), f32),
            pltpu.VMEM((16, FFM), f32),
            pltpu.VMEM((N_SEQ, N_DP, RANK, LANES), SEND),
            pltpu.VMEM((N_SEQ - 1, N_DP, RANK, LANES), SEND),
            pltpu.VMEM((N_DP, RANK, LANES), SEND),
            pltpu.VMEM((N_DP, RANK, LANES), SEND),
            pltpu.VMEM((N_DP, RANK, LANES), f32),
            pltpu.VMEM((2 * N_SEQ * N_MP, 1, LANES), f32),
            pltpu.VMEM((N_Z, 1, LANES), f32),
            sem((2,)),
            sem((CHUNKS,)),
            sem((3,)),
        ]
        + [sem] * 10
        + [pltpu.SemaphoreType.REGULAR((N_Z,))],
        compiler_params=pltpu.CompilerParams(
            collective_id=0, has_side_effects=True, vmem_limit_bytes=60 << 20
        ),
    )(hidden, cotangent, frozen_down.T, adapter.reshape(RANK, COLS), prior.reshape(1, NDOM), domain_of)
    out, log_new = pl.pallas_call(
        tail,
        out_shape=(
            jax.ShapeDtypeStruct((RANK, COLS), f32),
            jax.ShapeDtypeStruct((1, NDOM), f32),
        ),
        in_specs=[pl.BlockSpec(memory_space=pltpu.VMEM)] * 2,
        out_specs=(pl.BlockSpec(memory_space=pltpu.VMEM),) * 2,
    )(out, log_new)
    return out.reshape(1, RANK, COLS), log_new.reshape(NDOM)


def solution(mesh):
    return jax.shard_map(
        body,
        mesh=mesh,
        in_specs=(
            P(("dp", "seq"), "mp"),
            P(("dp", "seq"), "mp"),
            P("mp", None),
            P("mp", None, ("dp", "seq")),
            P(),
            P("dp"),
        ),
        out_specs=(P("mp", None, ("dp", "seq")), P()),
        check_vma=False,
    )
```

```python
import functools

import jax
import jax.numpy as jnp
from jax import lax
from jax.experimental import pallas as pl
from jax.experimental.pallas import tpu as pltpu
from jax.sharding import PartitionSpec as P

FF = 17920
NDOM = 48
RANK = 4
ROWS = 256
PIECE = 128
DM = 1664
FFM = 4480
N_DP = 32
N_SEQ = 4
N_MP = 4
COLS = FFM // (N_DP * N_SEQ)
LANES = 128
HALF = 64
CHUNKS = 2
SPAN = N_DP // CHUNKS
EDGES = tuple(min(c * 2304, FFM) for c in range(CHUNKS + 1))

SEND = jnp.bfloat16
N_Z = 16
SCORERS = (0, 1, 2, 3, 15, 14, 13, 12)
ORDER = (0, 1, 2, 3, 4, 5, 6, 7, 15, 8, 14, 9, 13, 10, 12, 11)
MESH = pl.DeviceIdType.MESH
step_rate = 1.0
learn_rate = 0.5


def kernel(
    hid_hbm, cot_hbm, fro_hbm, ada_hbm, pri_hbm, dom_hbm,
    out_ref, log_ref,
    hid, cot, fro, ada, pri, dom, wrow, part, lhs, g, spread, seqbuf, total, got, gotf, rows_a, rows_b,
    in_sem, cot_sem, small_sem, s1, r1, s2, r2, s3, r3, s4, r4, s5, r5, s6, r6, ready,
):
    dp, seq, mp = lax.axis_index("dp"), lax.axis_index("seq"), lax.axis_index("mp")

    def to(d=0, s=0, m=0):
        return {
            "dp": lax.rem(dp + d, N_DP),
            "seq": lax.rem(seq + s, N_SEQ),
            "mp": lax.rem(mp + m, N_MP),
        }

    z = lax.rem(dp, N_Z)
    place = jnp.where(z < 8, z, jnp.where(z < 12, 2 * z - 7, 38 - 2 * z))

    scorer = (z < 4) | (z >= 12)
    second = jnp.where(z < 4, z + 4, z - 4)

    def at(d):
        return {"dp": d, "seq": seq, "mp": mp}

    def send(src, dst, ssem, rsem, target=None, **where):
        copy = pltpu.make_async_remote_copy(
            src_ref=src, dst_ref=dst, send_sem=ssem, recv_sem=rsem,
            device_id=to(**where) if target is None else target, device_id_type=MESH,
        )
        copy.start()

    def done(ref, ssem, rsem, **where):
        return pltpu.make_async_remote_copy(
            src_ref=ref, dst_ref=ref, send_sem=ssem, recv_sem=rsem,
            device_id=to(**where), device_id_type=MESH,
        )

    loads = [
        pltpu.make_async_copy(fro_hbm, fro, in_sem.at[0]),
        pltpu.make_async_copy(hid_hbm, hid, in_sem.at[1]),
    ]
    for load in loads:
        load.start()
    barrier = pltpu.get_barrier_semaphore()
    plane = [(s, m) for s in (2, 1, 3, 0) for m in (2, 3, 1, 0) if (s, m) != (0, 0)]
    near = [(0, m) for m in range(1, N_MP)] + [(s, 0) for s in range(1, N_SEQ)]
    for s, m in near:
        pl.semaphore_signal(barrier, inc=1, device_id=to(s=s, m=m), device_id_type=MESH)
    pl.semaphore_signal(barrier, inc=1, device_id=to(d=N_Z), device_id_type=MESH)
    for position, plane_z in enumerate(ORDER):

        @pl.when(place < position)
        def _():
            for x in range(2):
                pl.semaphore_signal(barrier, inc=1, device_id=at(x * N_Z + plane_z), device_id_type=MESH)


    lhs[...] = jnp.zeros_like(lhs)
    wrow[...] = jnp.zeros_like(wrow)

    for load in loads:
        load.wait()
    cot_loads = []
    for c in range(CHUNKS):
        cut = pl.ds(EDGES[c], EDGES[c + 1] - EDGES[c])
        load = pltpu.make_async_copy(cot_hbm.at[:, cut], cot.at[:, cut], cot_sem.at[c])
        load.start()
        cot_loads.append(load)
    small = [
        pltpu.make_async_copy(ada_hbm, ada, small_sem.at[0]),
        pltpu.make_async_copy(pri_hbm, pri, small_sem.at[1]),
        pltpu.make_async_copy(dom_hbm, dom, small_sem.at[2]),
    ]
    for load in small:
        load.start()

    partial = lax.dot_general(
        fro[...], hid[...], (((1,), (1,)), ((), ())), preferred_element_type=jnp.float32
    )
    part[0] = partial.astype(jnp.bfloat16).astype(jnp.float32)

    pl.semaphore_wait(barrier, len(near) + 1 + 2 * place)
    for position, plane_z in enumerate(ORDER):

        @pl.when(place > position)
        def _():
            for x in range(2):
                pl.semaphore_signal(
                    ready.at[z], inc=1, device_id=at(x * N_Z + plane_z), device_id_type=MESH
                )

    for m in range(1, N_MP):
        send(part.at[0], part.at[m], s1, r1, m=m)
    done(part.at[pl.ds(1, N_MP - 1)], s1, r1, m=1).wait_recv()
    down = part[0] + part[1] + part[2] + part[3]
    token = lax.broadcasted_iota(jnp.int32, (RANK, ROWS), 1)
    lhs[0:RANK] = jnp.where(token < PIECE, down, 0.0)
    lhs[8 : 8 + RANK] = jnp.where(token < PIECE, 0.0, down)
    left = lhs[...].astype(jnp.bfloat16)
    lane = lax.broadcasted_iota(jnp.int32, (8, LANES), 1)
    for c in range(CHUNKS):
        cut = slice(EDGES[c], EDGES[c + 1])
        cot_loads[c].wait()
        g[:, cut] = jnp.dot(left, cot[:, cut], preferred_element_type=jnp.float32)
        for p in range(c * SPAN * N_SEQ, (c + 1) * SPAN * N_SEQ):
            v, o = divmod(p * COLS, LANES)
            a = g[0:8, v * LANES : (v + 1) * LANES]
            b = g[8:16, v * LANES : (v + 1) * LANES]
            a = a if o == 0 else pltpu.roll(a, LANES - o, 1)
            b = pltpu.roll(b, (HALF - o) % LANES, 1) if o != HALF else b
            if o + COLS > LANES:
                a2 = g[0:8, (v + 1) * LANES : (v + 2) * LANES]
                b2 = g[8:16, (v + 1) * LANES : (v + 2) * LANES]
                a2 = pltpu.roll(a2, LANES - o, 1)
                b2 = pltpu.roll(b2, (HALF - o) % LANES, 1) if o != HALF else b2
                a = jnp.where(lane < LANES - o, a, a2)
                b = jnp.where(lane < HALF + LANES - o, b, b2)
            joined = jnp.where(lane < HALF, a, b)
            spread[p % N_SEQ, p // N_SEQ] = joined[0:RANK].astype(SEND)
        part_of = pl.ds(c * SPAN, SPAN)
        for s in (2, 1, 3):
            send(spread.at[lax.rem(seq + s, N_SEQ), part_of], seqbuf.at[s - 1, part_of], s2, r2, s=s)

    for load in small:
        load.wait()
    d0 = dom[0].astype(jnp.float32)
    d1 = dom[1].astype(jnp.float32)
    done(seqbuf, s2, r2, s=1).wait_recv()
    f32 = jnp.float32
    summed = (
        spread[seq].astype(f32) + seqbuf[0].astype(f32) + seqbuf[1].astype(f32) + seqbuf[2].astype(f32)
    )
    lane3 = lax.broadcasted_iota(jnp.int32, (N_DP, RANK, LANES), 2)
    summed = jnp.where(lane3 == COLS, d0, jnp.where(lane3 == HALF + COLS, d1, summed))
    total[...] = summed.astype(SEND)

    def exchange(plane_z, scored):
        position = ORDER.index(plane_z)

        @pl.when(place < position)
        def _():
            pl.semaphore_wait(ready.at[plane_z], 2)

        @pl.when(place != position)
        def _():
            for x in range(2):
                d = x * N_Z + plane_z
                if scored:
                    other = d + 4 if plane_z < 4 else d - 4
                    send(total.at[other], got.at[1, dp], s6, r6, target=at(d))
                send(total.at[d], got.at[0, dp], s3, r3, target=at(d))

    base = dp - z
    partner = lax.rem(dp + N_Z, N_DP)
    for plane_z in SCORERS:
        exchange(plane_z, True)

    @pl.when(scorer)
    def _():
        send(total.at[partner - z + second], got.at[1, dp], s6, r6, target=at(partner))
        got[1, dp] = total[base + second]

    send(total.at[partner], got.at[0, dp], s3, r3, target=at(partner))
    got[0, dp] = total[dp]
    for plane_z in ORDER:
        if plane_z not in SCORERS:
            exchange(plane_z, False)

    wrow[:, 0:NDOM] = pri[...]
    prior = wrow[...]
    weights = prior / jnp.sum(prior, axis=1, keepdims=True)
    lane1 = lax.broadcasted_iota(jnp.int32, (1, LANES), 1)
    lane2 = lax.broadcasted_iota(jnp.int32, (N_DP, LANES), 1)
    low = lane2 < HALF

    done(got.at[0, pl.ds(0, N_DP - 1)], s3, r3, d=1).wait_recv()
    gotf[0] = got[0].astype(f32)
    rank_rows = [gotf[0, :, r, :] for r in range(RANK)]
    dom0 = rank_rows[0][:, COLS : COLS + 1]
    dom1 = rank_rows[0][:, HALF + COLS : HALF + COLS + 1]
    lanef = lane2.astype(f32)
    hot0 = (lanef == dom0).astype(f32)
    hot1 = (lanef == dom1).astype(f32)

    def per_sequence(row):
        return jnp.where(
            low,
            jnp.sum(hot0 * row, axis=1, keepdims=True),
            jnp.sum(hot1 * row, axis=1, keepdims=True),
        )

    def combine(scale, block):
        sums = [jnp.sum(scale * x, axis=0, keepdims=True) for x in block]
        return [x + pltpu.roll(x, HALF, 1) for x in sums]

    @pl.when(scorer)
    def _():
        done(got.at[1, pl.ds(0, N_DP - 1)], s6, r6, d=1).wait_recv()
        gotf[1] = got[1].astype(f32)
        second_rows = [gotf[1, :, r, :] for r in range(RANK)]
        valid = (lane1 < COLS) | ((lane1 >= HALF) & (lane1 < HALF + COLS))
        mine_w = per_sequence(weights)
        square = jnp.zeros((1, LANES), f32)
        product = jnp.zeros((N_DP, LANES), f32)
        for block in (rank_rows, second_rows):
            mixture = [jnp.where(valid, x, 0.0) for x in combine(mine_w, block)]
            square += sum(x * x for x in mixture)
            product += sum(x * y for x, y in zip(block, mixture))
        sumsq = jnp.sum(jnp.where(lane1 < HALF, square, 0.0), axis=1, keepdims=True)
        score0 = jnp.sum(jnp.where(low, product, 0.0), axis=1, keepdims=True)
        score1 = jnp.sum(jnp.where(low, 0.0, product), axis=1, keepdims=True)
        row = jnp.sum(hot0 * score0 + hot1 * score1, axis=0, keepdims=True)
        row = jnp.where(lane1 == LANES - 1, sumsq, row)
        mine = (dp // N_Z * N_SEQ + seq) * N_MP + mp
        rows_a[mine] = row
        slab = [(d, s, m) for s in (2, 1, 3, 0) for d in (N_Z, 0) for m in (2, 3, 1, 0)][:-1]
        for d, s, m in slab:
            send(rows_a.at[mine], rows_a.at[mine], s4, r4, d=d, s=s, m=m)
        done(rows_a.at[pl.ds(0, len(slab))], s4, r4, s=1).wait_recv()
        slot = jnp.where(z < 4, z, z - 8)
        rows_b[slot] = jnp.sum(rows_a[...], axis=0)
        for plane_z in (0, 1, 2, 3, 4, 5, 6, 7, 8, 15, 14, 9, 13, 10, 12, 11):

            @pl.when(z != plane_z)
            def _():
                send(rows_b.at[slot], rows_b.at[slot], s5, r5, target=at(base + plane_z))

        done(rows_b.at[pl.ds(0, len(SCORERS) - 1)], s5, r5, d=1).wait_recv()
        done(rows_a.at[pl.ds(0, len(slab))], s4, r4, s=1).wait_send()
        done(rows_a.at[pl.ds(0, N_Z - 1)], s5, r5, d=1).wait_send()
        done(got.at[1, pl.ds(0, len(SCORERS) * 2 - 1)], s6, r6, d=1).wait_send()

    @pl.when(jnp.logical_not(scorer))
    def _():
        done(rows_b, s5, r5, d=1).wait_recv()
        done(got.at[1, pl.ds(0, len(SCORERS) * 2)], s6, r6, d=1).wait_send()

    row = jnp.sum(rows_b[...], axis=0)

    sumsq = jnp.sum(jnp.where(lane1 == LANES - 1, row, 0.0), axis=1, keepdims=True)
    scores = jnp.where(lane1 < NDOM, row, 0.0)
    meansq = sumsq / (RANK * FF) + 1e-06
    ratio = scores / (RANK * FF * meansq)
    raised = weights * jnp.exp(step_rate * ratio)
    log_new = jnp.log(weights) + step_rate * ratio - jnp.log(jnp.sum(raised, axis=1, keepdims=True))
    log_ref[...] = log_new[:, 0:NDOM]
    new = jnp.where(lane1 < NDOM, jnp.exp(log_new), 0.0)
    update = combine(per_sequence(new), rank_rows)
    root = jnp.sqrt(meansq)
    for r in range(RANK):
        moved = learn_rate * update[r] / root
        out_ref[r : r + 1, :] = ada[r : r + 1, :] - moved[:, 0:COLS]

    done(part.at[pl.ds(1, N_MP - 1)], s1, r1, m=1).wait_send()
    done(seqbuf, s2, r2, s=1).wait_send()
    done(got.at[0, pl.ds(0, N_DP - 1)], s3, r3, d=1).wait_send()


def tail(moved, log_new, out_ref, log_ref):
    out_ref[...] = moved[...]
    log_ref[...] = log_new[...]


def body(hidden, cotangent, frozen_down, adapter, prior, domain_of):
    f32 = jnp.float32
    sem = pltpu.SemaphoreType.DMA
    out, log_new = pl.pallas_call(
        kernel,
        out_shape=(
            jax.ShapeDtypeStruct((RANK, COLS), f32),
            jax.ShapeDtypeStruct((1, NDOM), f32),
        ),
        in_specs=[pl.BlockSpec(memory_space=pl.ANY)] * 6,
        out_specs=(pl.BlockSpec(memory_space=pltpu.VMEM),) * 2,
        scratch_shapes=[
            pltpu.VMEM((ROWS, DM), jnp.bfloat16),
            pltpu.VMEM((ROWS, FFM), jnp.bfloat16),
            pltpu.VMEM((RANK, DM), jnp.bfloat16),
            pltpu.VMEM((RANK, COLS), f32),
            pltpu.VMEM((1, NDOM), f32),
            pltpu.SMEM((2,), jnp.int32),
            pltpu.VMEM((1, LANES), f32),
            pltpu.VMEM((N_MP, RANK, ROWS), f32),
            pltpu.VMEM((16, ROWS), f32),
            pltpu.VMEM((16, FFM), f32),
            pltpu.VMEM((N_SEQ, N_DP, RANK, LANES), SEND),
            pltpu.VMEM((N_SEQ - 1, N_DP, RANK, LANES), SEND),
            pltpu.VMEM((N_DP, RANK, LANES), SEND),
            pltpu.VMEM((2, N_DP, RANK, LANES), SEND),
            pltpu.VMEM((2, N_DP, RANK, LANES), f32),
            pltpu.VMEM((2 * N_SEQ * N_MP, 1, LANES), f32),
            pltpu.VMEM((len(SCORERS), 1, LANES), f32),
            sem((2,)),
            sem((CHUNKS,)),
            sem((3,)),
        ]
        + [sem] * 12
        + [pltpu.SemaphoreType.REGULAR((N_Z,))],
        compiler_params=pltpu.CompilerParams(
            collective_id=0, has_side_effects=True, vmem_limit_bytes=60 << 20
        ),
    )(hidden, cotangent, frozen_down.T, adapter.reshape(RANK, COLS), prior.reshape(1, NDOM), domain_of)
    out, log_new = pl.pallas_call(
        tail,
        out_shape=(
            jax.ShapeDtypeStruct((RANK, COLS), f32),
            jax.ShapeDtypeStruct((1, NDOM), f32),
        ),
        in_specs=[pl.BlockSpec(memory_space=pltpu.VMEM)] * 2,
        out_specs=(pl.BlockSpec(memory_space=pltpu.VMEM),) * 2,
    )(out, log_new)
    return out.reshape(1, RANK, COLS), log_new.reshape(NDOM)


def solution(mesh):
    return jax.shard_map(
        body,
        mesh=mesh,
        in_specs=(
            P(("dp", "seq"), "mp"),
            P(("dp", "seq"), "mp"),
            P("mp", None),
            P("mp", None, ("dp", "seq")),
            P(),
            P("dp"),
        ),
        out_specs=(P("mp", None, ("dp", "seq")), P()),
        check_vma=False,
    )
```

```python
import functools

import jax
import jax.numpy as jnp
from jax import lax
from jax.experimental import pallas as pl
from jax.experimental.pallas import tpu as pltpu
from jax.sharding import PartitionSpec as P

FF = 17920
NDOM = 48
RANK = 4
ROWS = 256
PIECE = 128
DM = 1664
FFM = 4480
N_DP = 32
N_SEQ = 4
N_MP = 4
COLS = FFM // (N_DP * N_SEQ)
LANES = 128
HALF = 64
CHUNKS = 2
SPAN = N_DP // CHUNKS
EDGES = tuple(min(c * 2304, FFM) for c in range(CHUNKS + 1))

SEND = jnp.bfloat16
N_Z = 16
SIDE = 4
BLOCKS = N_Z // (2 * SIDE)
SCORERS = (0, 1, 2, 3, 15, 14, 13, 12)
ORDER = (0, 1, 2, 3, 4, 5, 6, 7, 15, 8, 14, 9, 13, 10, 12, 11)
MESH = pl.DeviceIdType.MESH
step_rate = 1.0
learn_rate = 0.5


def kernel(
    hid_hbm, cot_hbm, fro_hbm, ada_hbm, pri_hbm, dom_hbm,
    out_ref, log_ref,
    hid, cot, fro, ada, pri, dom, wrow, part, lhs, g, spread, seqbuf, total, got, gotf, rows_a, rows_b,
    in_sem, cot_sem, small_sem, s1, r1, s2, r2, s3, r3, s4, r4, s5, r5, s6, r6, ready,
):
    dp, seq, mp = lax.axis_index("dp"), lax.axis_index("seq"), lax.axis_index("mp")

    def to(d=0, s=0, m=0):
        return {
            "dp": lax.rem(dp + d, N_DP),
            "seq": lax.rem(seq + s, N_SEQ),
            "mp": lax.rem(mp + m, N_MP),
        }

    z = lax.rem(dp, N_Z)
    place = jnp.where(z < 8, z, jnp.where(z < 12, 2 * z - 7, 38 - 2 * z))

    scorer = (z < SIDE) | (z >= N_Z - SIDE)
    stride = jnp.where(z < SIDE, SIDE, -SIDE)

    def at(d):
        return {"dp": d, "seq": seq, "mp": mp}

    def send(src, dst, ssem, rsem, target=None, **where):
        copy = pltpu.make_async_remote_copy(
            src_ref=src, dst_ref=dst, send_sem=ssem, recv_sem=rsem,
            device_id=to(**where) if target is None else target, device_id_type=MESH,
        )
        copy.start()

    def done(ref, ssem, rsem, **where):
        return pltpu.make_async_remote_copy(
            src_ref=ref, dst_ref=ref, send_sem=ssem, recv_sem=rsem,
            device_id=to(**where), device_id_type=MESH,
        )

    loads = [
        pltpu.make_async_copy(fro_hbm, fro, in_sem.at[0]),
        pltpu.make_async_copy(hid_hbm, hid, in_sem.at[1]),
    ]
    for load in loads:
        load.start()
    barrier = pltpu.get_barrier_semaphore()
    plane = [(s, m) for s in (2, 1, 3, 0) for m in (2, 3, 1, 0) if (s, m) != (0, 0)]
    near = [(0, m) for m in range(1, N_MP)] + [(s, 0) for s in range(1, N_SEQ)]
    for s, m in near:
        pl.semaphore_signal(barrier, inc=1, device_id=to(s=s, m=m), device_id_type=MESH)
    pl.semaphore_signal(barrier, inc=1, device_id=to(d=N_Z), device_id_type=MESH)
    for position, plane_z in enumerate(ORDER):

        @pl.when(place < position)
        def _():
            for x in range(2):
                pl.semaphore_signal(barrier, inc=1, device_id=at(x * N_Z + plane_z), device_id_type=MESH)


    lhs[...] = jnp.zeros_like(lhs)
    wrow[...] = jnp.zeros_like(wrow)

    for load in loads:
        load.wait()
    cot_loads = []
    for c in range(CHUNKS):
        cut = pl.ds(EDGES[c], EDGES[c + 1] - EDGES[c])
        load = pltpu.make_async_copy(cot_hbm.at[:, cut], cot.at[:, cut], cot_sem.at[c])
        load.start()
        cot_loads.append(load)
    small = [
        pltpu.make_async_copy(ada_hbm, ada, small_sem.at[0]),
        pltpu.make_async_copy(pri_hbm, pri, small_sem.at[1]),
        pltpu.make_async_copy(dom_hbm, dom, small_sem.at[2]),
    ]
    for load in small:
        load.start()

    partial = lax.dot_general(
        fro[...], hid[...], (((1,), (1,)), ((), ())), preferred_element_type=jnp.float32
    )
    part[0] = partial.astype(jnp.bfloat16).astype(jnp.float32)

    pl.semaphore_wait(barrier, len(near) + 1 + 2 * place)
    for position, plane_z in enumerate(ORDER):

        @pl.when(place > position)
        def _():
            for x in range(2):
                pl.semaphore_signal(
                    ready.at[z], inc=1, device_id=at(x * N_Z + plane_z), device_id_type=MESH
                )

    for m in range(1, N_MP):
        send(part.at[0], part.at[m], s1, r1, m=m)
    done(part.at[pl.ds(1, N_MP - 1)], s1, r1, m=1).wait_recv()
    down = part[0] + part[1] + part[2] + part[3]
    token = lax.broadcasted_iota(jnp.int32, (RANK, ROWS), 1)
    lhs[0:RANK] = jnp.where(token < PIECE, down, 0.0)
    lhs[8 : 8 + RANK] = jnp.where(token < PIECE, 0.0, down)
    left = lhs[...].astype(jnp.bfloat16)
    lane = lax.broadcasted_iota(jnp.int32, (8, LANES), 1)
    for c in range(CHUNKS):
        cut = slice(EDGES[c], EDGES[c + 1])
        cot_loads[c].wait()
        g[:, cut] = jnp.dot(left, cot[:, cut], preferred_element_type=jnp.float32)
        for p in range(c * SPAN * N_SEQ, (c + 1) * SPAN * N_SEQ):
            v, o = divmod(p * COLS, LANES)
            a = g[0:8, v * LANES : (v + 1) * LANES]
            b = g[8:16, v * LANES : (v + 1) * LANES]
            a = a if o == 0 else pltpu.roll(a, LANES - o, 1)
            b = pltpu.roll(b, (HALF - o) % LANES, 1) if o != HALF else b
            if o + COLS > LANES:
                a2 = g[0:8, (v + 1) * LANES : (v + 2) * LANES]
                b2 = g[8:16, (v + 1) * LANES : (v + 2) * LANES]
                a2 = pltpu.roll(a2, LANES - o, 1)
                b2 = pltpu.roll(b2, (HALF - o) % LANES, 1) if o != HALF else b2
                a = jnp.where(lane < LANES - o, a, a2)
                b = jnp.where(lane < HALF + LANES - o, b, b2)
            joined = jnp.where(lane < HALF, a, b)
            spread[p % N_SEQ, p // N_SEQ] = joined[0:RANK].astype(SEND)
        part_of = pl.ds(c * SPAN, SPAN)
        for s in (2, 1, 3):
            send(spread.at[lax.rem(seq + s, N_SEQ), part_of], seqbuf.at[s - 1, part_of], s2, r2, s=s)

    for load in small:
        load.wait()
    d0 = dom[0].astype(jnp.float32)
    d1 = dom[1].astype(jnp.float32)
    done(seqbuf, s2, r2, s=1).wait_recv()
    f32 = jnp.float32
    summed = (
        spread[seq].astype(f32) + seqbuf[0].astype(f32) + seqbuf[1].astype(f32) + seqbuf[2].astype(f32)
    )
    lane3 = lax.broadcasted_iota(jnp.int32, (N_DP, RANK, LANES), 2)
    summed = jnp.where(lane3 == COLS, d0, jnp.where(lane3 == HALF + COLS, d1, summed))
    total[...] = summed.astype(SEND)

    def exchange(plane_z, scored):
        position = ORDER.index(plane_z)

        @pl.when(place < position)
        def _():
            pl.semaphore_wait(ready.at[plane_z], 2)

        @pl.when(place != position)
        def _():
            for x in range(2):
                d = x * N_Z + plane_z
                if scored:
                    step = SIDE if plane_z < SIDE else -SIDE
                    for k in range(1, BLOCKS):
                        send(total.at[d + k * step], got.at[k, dp], s6, r6, target=at(d))
                send(total.at[d], got.at[0, dp], s3, r3, target=at(d))

    base = dp - z
    partner = lax.rem(dp + N_Z, N_DP)
    for plane_z in SCORERS:
        exchange(plane_z, True)

    @pl.when(scorer)
    def _():
        for k in range(1, BLOCKS):
            send(total.at[partner + k * stride], got.at[k, dp], s6, r6, target=at(partner))
            got[k, dp] = total[dp + k * stride]

    send(total.at[partner], got.at[0, dp], s3, r3, target=at(partner))
    got[0, dp] = total[dp]
    def rest():
        for plane_z in ORDER:
            if plane_z not in SCORERS:
                exchange(plane_z, False)

    pl.when(jnp.logical_not(scorer))(rest)
    wrow[:, 0:NDOM] = pri[...]
    prior = wrow[...]
    weights = prior / jnp.sum(prior, axis=1, keepdims=True)
    lane1 = lax.broadcasted_iota(jnp.int32, (1, LANES), 1)
    lane2 = lax.broadcasted_iota(jnp.int32, (N_DP, LANES), 1)
    low = lane2 < HALF

    done(got.at[0, pl.ds(0, N_DP - 1)], s3, r3, d=1).wait_recv()
    gotf[0] = got[0].astype(f32)
    rank_rows = [gotf[0, :, r, :] for r in range(RANK)]
    dom0 = rank_rows[0][:, COLS : COLS + 1]
    dom1 = rank_rows[0][:, HALF + COLS : HALF + COLS + 1]
    lanef = lane2.astype(f32)
    hot0 = (lanef == dom0).astype(f32)
    hot1 = (lanef == dom1).astype(f32)

    def per_sequence(row):
        return jnp.where(
            low,
            jnp.sum(hot0 * row, axis=1, keepdims=True),
            jnp.sum(hot1 * row, axis=1, keepdims=True),
        )

    def combine(scale, block):
        sums = [jnp.sum(scale * x, axis=0, keepdims=True) for x in block]
        return [x + pltpu.roll(x, HALF, 1) for x in sums]

    @pl.when(scorer)
    def _():
        others = got.at[pl.ds(1, BLOCKS - 1), pl.ds(0, N_DP - 1)]
        done(others, s6, r6, d=1).wait_recv()
        blocks = [rank_rows]
        for k in range(1, BLOCKS):
            gotf[k] = got[k].astype(f32)
            blocks.append([gotf[k, :, r, :] for r in range(RANK)])
        valid = (lane1 < COLS) | ((lane1 >= HALF) & (lane1 < HALF + COLS))
        mine_w = per_sequence(weights)
        square = jnp.zeros((1, LANES), f32)
        product = jnp.zeros((N_DP, LANES), f32)
        for block in blocks:
            mixture = [jnp.where(valid, x, 0.0) for x in combine(mine_w, block)]
            square += sum(x * x for x in mixture)
            product += sum(x * y for x, y in zip(block, mixture))
        sumsq = jnp.sum(jnp.where(lane1 < HALF, square, 0.0), axis=1, keepdims=True)
        score0 = jnp.sum(jnp.where(low, product, 0.0), axis=1, keepdims=True)
        score1 = jnp.sum(jnp.where(low, 0.0, product), axis=1, keepdims=True)
        row = jnp.sum(hot0 * score0 + hot1 * score1, axis=0, keepdims=True)
        row = jnp.where(lane1 == LANES - 1, sumsq, row)
        mine = (dp // N_Z * N_SEQ + seq) * N_MP + mp
        rows_a[mine] = row
        slab = [(d, s, m) for s in (2, 1, 3, 0) for d in (N_Z, 0) for m in (2, 3, 1, 0)][:-1]
        for d, s, m in slab:
            send(rows_a.at[mine], rows_a.at[mine], s4, r4, d=d, s=s, m=m)
        done(rows_a.at[pl.ds(0, len(slab))], s4, r4, s=1).wait_recv()
        slot = jnp.where(z < SIDE, z, z - (N_Z - 2 * SIDE))
        rows_b[slot] = jnp.sum(rows_a[...], axis=0)
        for plane_z in (0, 1, 2, 3, 4, 5, 6, 7, 8, 15, 14, 9, 13, 10, 12, 11):

            @pl.when(z != plane_z)
            def _():
                send(rows_b.at[slot], rows_b.at[slot], s5, r5, target=at(base + plane_z))

        rest()
        done(rows_b.at[pl.ds(0, len(SCORERS) - 1)], s5, r5, d=1).wait_recv()
        done(rows_a.at[pl.ds(0, len(slab))], s4, r4, s=1).wait_send()
        done(rows_a.at[pl.ds(0, N_Z - 1)], s5, r5, d=1).wait_send()
        sent = got.at[pl.ds(1, BLOCKS - 1), pl.ds(0, len(SCORERS) * 2 - 1)]
        done(sent, s6, r6, d=1).wait_send()

    @pl.when(jnp.logical_not(scorer))
    def _():
        done(rows_b, s5, r5, d=1).wait_recv()
        sent = got.at[pl.ds(1, BLOCKS - 1), pl.ds(0, len(SCORERS) * 2)]
        done(sent, s6, r6, d=1).wait_send()

    row = jnp.sum(rows_b[...], axis=0)

    sumsq = jnp.sum(jnp.where(lane1 == LANES - 1, row, 0.0), axis=1, keepdims=True)
    scores = jnp.where(lane1 < NDOM, row, 0.0)
    meansq = sumsq / (RANK * FF) + 1e-06
    ratio = scores / (RANK * FF * meansq)
    raised = weights * jnp.exp(step_rate * ratio)
    log_new = jnp.log(weights) + step_rate * ratio - jnp.log(jnp.sum(raised, axis=1, keepdims=True))
    log_ref[...] = log_new[:, 0:NDOM]
    new = jnp.where(lane1 < NDOM, jnp.exp(log_new), 0.0)
    update = combine(per_sequence(new), rank_rows)
    root = jnp.sqrt(meansq)
    for r in range(RANK):
        moved = learn_rate * update[r] / root
        out_ref[r : r + 1, :] = ada[r : r + 1, :] - moved[:, 0:COLS]

    done(part.at[pl.ds(1, N_MP - 1)], s1, r1, m=1).wait_send()
    done(seqbuf, s2, r2, s=1).wait_send()
    done(got.at[0, pl.ds(0, N_DP - 1)], s3, r3, d=1).wait_send()


def tail(moved, log_new, out_ref, log_ref):
    out_ref[...] = moved[...]
    log_ref[...] = log_new[...]


def body(hidden, cotangent, frozen_down, adapter, prior, domain_of):
    f32 = jnp.float32
    sem = pltpu.SemaphoreType.DMA
    out, log_new = pl.pallas_call(
        kernel,
        out_shape=(
            jax.ShapeDtypeStruct((RANK, COLS), f32),
            jax.ShapeDtypeStruct((1, NDOM), f32),
        ),
        in_specs=[pl.BlockSpec(memory_space=pl.ANY)] * 6,
        out_specs=(pl.BlockSpec(memory_space=pltpu.VMEM),) * 2,
        scratch_shapes=[
            pltpu.VMEM((ROWS, DM), jnp.bfloat16),
            pltpu.VMEM((ROWS, FFM), jnp.bfloat16),
            pltpu.VMEM((RANK, DM), jnp.bfloat16),
            pltpu.VMEM((RANK, COLS), f32),
            pltpu.VMEM((1, NDOM), f32),
            pltpu.SMEM((2,), jnp.int32),
            pltpu.VMEM((1, LANES), f32),
            pltpu.VMEM((N_MP, RANK, ROWS), f32),
            pltpu.VMEM((16, ROWS), f32),
            pltpu.VMEM((16, FFM), f32),
            pltpu.VMEM((N_SEQ, N_DP, RANK, LANES), SEND),
            pltpu.VMEM((N_SEQ - 1, N_DP, RANK, LANES), SEND),
            pltpu.VMEM((N_DP, RANK, LANES), SEND),
            pltpu.VMEM((BLOCKS, N_DP, RANK, LANES), SEND),
            pltpu.VMEM((BLOCKS, N_DP, RANK, LANES), f32),
            pltpu.VMEM((2 * N_SEQ * N_MP, 1, LANES), f32),
            pltpu.VMEM((len(SCORERS), 1, LANES), f32),
            sem((2,)),
            sem((CHUNKS,)),
            sem((3,)),
        ]
        + [sem] * 12
        + [pltpu.SemaphoreType.REGULAR((N_Z,))],
        compiler_params=pltpu.CompilerParams(
            collective_id=0, has_side_effects=True, vmem_limit_bytes=60 << 20
        ),
    )(hidden, cotangent, frozen_down.T, adapter.reshape(RANK, COLS), prior.reshape(1, NDOM), domain_of)
    out, log_new = pl.pallas_call(
        tail,
        out_shape=(
            jax.ShapeDtypeStruct((RANK, COLS), f32),
            jax.ShapeDtypeStruct((1, NDOM), f32),
        ),
        in_specs=[pl.BlockSpec(memory_space=pltpu.VMEM)] * 2,
        out_specs=(pl.BlockSpec(memory_space=pltpu.VMEM),) * 2,
    )(out, log_new)
    return out.reshape(1, RANK, COLS), log_new.reshape(NDOM)


def solution(mesh):
    return jax.shard_map(
        body,
        mesh=mesh,
        in_specs=(
            P(("dp", "seq"), "mp"),
            P(("dp", "seq"), "mp"),
            P("mp", None),
            P("mp", None, ("dp", "seq")),
            P(),
            P("dp"),
        ),
        out_specs=(P("mp", None, ("dp", "seq")), P()),
        check_vma=False,
    )
```

```python
import functools

import jax
import jax.numpy as jnp
from jax import lax
from jax.experimental import pallas as pl
from jax.experimental.pallas import tpu as pltpu
from jax.sharding import PartitionSpec as P

FF = 17920
NDOM = 48
RANK = 4
ROWS = 256
PIECE = 128
DM = 1664
FFM = 4480
N_DP = 32
N_SEQ = 4
N_MP = 4
COLS = FFM // (N_DP * N_SEQ)
LANES = 128
HALF = 64
CHUNKS = 2
SPAN = N_DP // CHUNKS
EDGES = tuple(min(c * 2304, FFM) for c in range(CHUNKS + 1))

SEND = jnp.bfloat16
N_Z = 16
SIDE = 2
EARLY = 4
SLAB = 32
BLOCKS = N_Z // (2 * SIDE)
SCORERS = (0, 1, 15, 14)
ORDER = (0, 1, 2, 3, 4, 5, 6, 7, 15, 8, 14, 9, 13, 10, 12, 11)
MESH = pl.DeviceIdType.MESH
step_rate = 1.0
learn_rate = 0.5


def kernel(
    hid_hbm, cot_hbm, fro_hbm, ada_hbm, pri_hbm, dom_hbm,
    out_ref, log_ref,
    hid, cot, fro, ada, pri, dom, wrow, part, lhs, g, spread, seqbuf, total, got, gotf, rows_a, rows_b,
    in_sem, cot_sem, small_sem, s1, r1, s2, r2, s3, r3, s4, r4, s5, r5, s6, r6, ready,
):
    dp, seq, mp = lax.axis_index("dp"), lax.axis_index("seq"), lax.axis_index("mp")

    def to(d=0, s=0, m=0):
        return {
            "dp": lax.rem(dp + d, N_DP),
            "seq": lax.rem(seq + s, N_SEQ),
            "mp": lax.rem(mp + m, N_MP),
        }

    z = lax.rem(dp, N_Z)
    place = jnp.where(z < 8, z, jnp.where(z < 12, 2 * z - 7, 38 - 2 * z))

    scorer = (z < SIDE) | (z >= N_Z - SIDE)
    stride = jnp.where(z < SIDE, SIDE, -SIDE)

    def at(d):
        return {"dp": d, "seq": seq, "mp": mp}

    def send(src, dst, ssem, rsem, target=None, **where):
        copy = pltpu.make_async_remote_copy(
            src_ref=src, dst_ref=dst, send_sem=ssem, recv_sem=rsem,
            device_id=to(**where) if target is None else target, device_id_type=MESH,
        )
        copy.start()

    def done(ref, ssem, rsem, **where):
        return pltpu.make_async_remote_copy(
            src_ref=ref, dst_ref=ref, send_sem=ssem, recv_sem=rsem,
            device_id=to(**where), device_id_type=MESH,
        )

    loads = [
        pltpu.make_async_copy(fro_hbm, fro, in_sem.at[0]),
        pltpu.make_async_copy(hid_hbm, hid, in_sem.at[1]),
    ]
    for load in loads:
        load.start()
    barrier = pltpu.get_barrier_semaphore()
    plane = [(s, m) for s in (2, 1, 3, 0) for m in (2, 3, 1, 0) if (s, m) != (0, 0)]
    near = [(0, m) for m in range(1, N_MP)] + [(s, 0) for s in range(1, N_SEQ)]
    for s, m in near:
        pl.semaphore_signal(barrier, inc=1, device_id=to(s=s, m=m), device_id_type=MESH)
    pl.semaphore_signal(barrier, inc=1, device_id=to(d=N_Z), device_id_type=MESH)
    for position, plane_z in enumerate(ORDER):

        @pl.when(place < position)
        def _():
            for x in range(2):
                pl.semaphore_signal(barrier, inc=1, device_id=at(x * N_Z + plane_z), device_id_type=MESH)


    lhs[...] = jnp.zeros_like(lhs)
    wrow[...] = jnp.zeros_like(wrow)

    for load in loads:
        load.wait()
    cot_loads = []
    for c in range(CHUNKS):
        cut = pl.ds(EDGES[c], EDGES[c + 1] - EDGES[c])
        load = pltpu.make_async_copy(cot_hbm.at[:, cut], cot.at[:, cut], cot_sem.at[c])
        load.start()
        cot_loads.append(load)
    small = [
        pltpu.make_async_copy(ada_hbm, ada, small_sem.at[0]),
        pltpu.make_async_copy(pri_hbm, pri, small_sem.at[1]),
        pltpu.make_async_copy(dom_hbm, dom, small_sem.at[2]),
    ]
    for load in small:
        load.start()

    partial = lax.dot_general(
        fro[...], hid[...], (((1,), (1,)), ((), ())), preferred_element_type=jnp.float32
    )
    part[0] = partial.astype(jnp.bfloat16).astype(jnp.float32)

    pl.semaphore_wait(barrier, len(near) + 1 + 2 * place)
    for position, plane_z in enumerate(ORDER):

        @pl.when(place > position)
        def _():
            for x in range(2):
                pl.semaphore_signal(
                    ready.at[z], inc=1, device_id=at(x * N_Z + plane_z), device_id_type=MESH
                )

    for m in range(1, N_MP):
        send(part.at[0], part.at[m], s1, r1, m=m)
    done(part.at[pl.ds(1, N_MP - 1)], s1, r1, m=1).wait_recv()
    down = part[0] + part[1] + part[2] + part[3]
    token = lax.broadcasted_iota(jnp.int32, (RANK, ROWS), 1)
    lhs[0:RANK] = jnp.where(token < PIECE, down, 0.0)
    lhs[8 : 8 + RANK] = jnp.where(token < PIECE, 0.0, down)
    left = lhs[...].astype(jnp.bfloat16)
    lane = lax.broadcasted_iota(jnp.int32, (8, LANES), 1)
    for c in range(CHUNKS):
        cut = slice(EDGES[c], EDGES[c + 1])
        cot_loads[c].wait()
        g[:, cut] = jnp.dot(left, cot[:, cut], preferred_element_type=jnp.float32)
        for p in range(c * SPAN * N_SEQ, (c + 1) * SPAN * N_SEQ):
            v, o = divmod(p * COLS, LANES)
            a = g[0:8, v * LANES : (v + 1) * LANES]
            b = g[8:16, v * LANES : (v + 1) * LANES]
            a = a if o == 0 else pltpu.roll(a, LANES - o, 1)
            b = pltpu.roll(b, (HALF - o) % LANES, 1) if o != HALF else b
            if o + COLS > LANES:
                a2 = g[0:8, (v + 1) * LANES : (v + 2) * LANES]
                b2 = g[8:16, (v + 1) * LANES : (v + 2) * LANES]
                a2 = pltpu.roll(a2, LANES - o, 1)
                b2 = pltpu.roll(b2, (HALF - o) % LANES, 1) if o != HALF else b2
                a = jnp.where(lane < LANES - o, a, a2)
                b = jnp.where(lane < HALF + LANES - o, b, b2)
            joined = jnp.where(lane < HALF, a, b)
            spread[p % N_SEQ, p // N_SEQ] = joined[0:RANK].astype(SEND)
        part_of = pl.ds(c * SPAN, SPAN)
        for s in (2, 1, 3):
            send(spread.at[lax.rem(seq + s, N_SEQ), part_of], seqbuf.at[s - 1, part_of], s2, r2, s=s)

    for load in small:
        load.wait()
    d0 = dom[0].astype(jnp.float32)
    d1 = dom[1].astype(jnp.float32)
    done(seqbuf, s2, r2, s=1).wait_recv()
    f32 = jnp.float32
    summed = (
        spread[seq].astype(f32) + seqbuf[0].astype(f32) + seqbuf[1].astype(f32) + seqbuf[2].astype(f32)
    )
    lane3 = lax.broadcasted_iota(jnp.int32, (N_DP, RANK, LANES), 2)
    summed = jnp.where(lane3 == COLS, d0, jnp.where(lane3 == HALF + COLS, d1, summed))
    total[...] = summed.astype(SEND)

    def exchange(plane_z, scored):
        position = ORDER.index(plane_z)

        @pl.when(place < position)
        def _():
            pl.semaphore_wait(ready.at[plane_z], 2)

        @pl.when(place != position)
        def _():
            for x in range(2):
                d = x * N_Z + plane_z
                if scored:
                    step = SIDE if plane_z < SIDE else -SIDE
                    for k in range(1, BLOCKS):
                        send(total.at[d + k * step], got.at[k, dp], s6, r6, target=at(d))
                send(total.at[d], got.at[0, dp], s3, r3, target=at(d))

    base = dp - z
    partner = lax.rem(dp + N_Z, N_DP)
    for plane_z in SCORERS:
        exchange(plane_z, True)

    @pl.when(scorer)
    def _():
        for k in range(1, BLOCKS):
            send(total.at[partner + k * stride], got.at[k, dp], s6, r6, target=at(partner))
            got[k, dp] = total[dp + k * stride]

    send(total.at[partner], got.at[0, dp], s3, r3, target=at(partner))
    got[0, dp] = total[dp]
    def rest():
        for plane_z in ORDER:
            if plane_z not in SCORERS:
                exchange(plane_z, False)

    pl.when(jnp.logical_not(scorer))(rest)
    wrow[:, 0:NDOM] = pri[...]
    prior = wrow[...]
    weights = prior / jnp.sum(prior, axis=1, keepdims=True)
    lane1 = lax.broadcasted_iota(jnp.int32, (1, LANES), 1)
    lane2 = lax.broadcasted_iota(jnp.int32, (N_DP, LANES), 1)
    low = lane2 < HALF

    done(got.at[0, pl.ds(0, N_DP - 1)], s3, r3, d=1).wait_recv()
    gotf[0] = got[0].astype(f32)
    rank_rows = [gotf[0, :, r, :] for r in range(RANK)]
    dom0 = rank_rows[0][:, COLS : COLS + 1]
    dom1 = rank_rows[0][:, HALF + COLS : HALF + COLS + 1]
    lanef = lane2.astype(f32)
    hot0 = (lanef == dom0).astype(f32)
    hot1 = (lanef == dom1).astype(f32)

    def per_sequence(row):
        return jnp.where(
            low,
            jnp.sum(hot0 * row, axis=1, keepdims=True),
            jnp.sum(hot1 * row, axis=1, keepdims=True),
        )

    def combine(scale, block):
        sums = [jnp.sum(scale * x, axis=0, keepdims=True) for x in block]
        return [x + pltpu.roll(x, HALF, 1) for x in sums]

    @pl.when(scorer)
    def _():
        others = got.at[pl.ds(1, BLOCKS - 1), pl.ds(0, N_DP - 1)]
        done(others, s6, r6, d=1).wait_recv()
        blocks = [rank_rows]
        for k in range(1, BLOCKS):
            gotf[k] = got[k].astype(f32)
            blocks.append([gotf[k, :, r, :] for r in range(RANK)])
        valid = (lane1 < COLS) | ((lane1 >= HALF) & (lane1 < HALF + COLS))
        mine_w = per_sequence(weights)
        square = jnp.zeros((1, LANES), f32)
        product = jnp.zeros((N_DP, LANES), f32)
        for block in blocks:
            mixture = [jnp.where(valid, x, 0.0) for x in combine(mine_w, block)]
            square += sum(x * x for x in mixture)
            product += sum(x * y for x, y in zip(block, mixture))
        sumsq = jnp.sum(jnp.where(lane1 < HALF, square, 0.0), axis=1, keepdims=True)
        score0 = jnp.sum(jnp.where(low, product, 0.0), axis=1, keepdims=True)
        score1 = jnp.sum(jnp.where(low, 0.0, product), axis=1, keepdims=True)
        row = jnp.sum(hot0 * score0 + hot1 * score1, axis=0, keepdims=True)
        row = jnp.where(lane1 == LANES - 1, sumsq, row)
        slot = jnp.where(z < SIDE, z, z - (N_Z - 2 * SIDE))
        mine = ((slot * 2 + dp // N_Z) * N_SEQ + seq) * N_MP + mp
        rows_a[mine] = row
        slab = [(d, s, m) for s in (2, 1, 3, 0) for d in (1, 0) for m in (2, 3, 1, 0)]

        @pl.loop(0, EARLY)
        def _(plane_z):
            for d, s, m in slab:
                target = {
                    "dp": lax.rem(dp // N_Z + d, 2) * N_Z + plane_z,
                    "seq": lax.rem(seq + s, N_SEQ),
                    "mp": lax.rem(mp + m, N_MP),
                }

                def push(target=target):
                    send(rows_a.at[mine], rows_a.at[mine], s4, r4, target=target)

                if (d, s, m) == (0, 0, 0):
                    pl.when(z != plane_z)(push)
                else:
                    push()

        rest()

    rows_in = 2 * SIDE * SLAB

    @pl.when(z < EARLY)
    def _():
        @pl.when(scorer)
        def _():
            done(rows_a.at[pl.ds(0, rows_in - 1)], s4, r4, d=1).wait_recv()

        @pl.when(jnp.logical_not(scorer))
        def _():
            done(rows_a, s4, r4, d=1).wait_recv()

        rows_b[0] = jnp.sum(rows_a[...], axis=0)

        @pl.when(z == 0)
        def _():
            for plane_z in (8, 7, 9, 6, 10, 5, 11, 4, 12, 13, 14, 15):
                send(rows_b.at[0], rows_b.at[0], s5, r5, target=at(base + plane_z))

    @pl.when(z >= EARLY)
    def _():
        done(rows_b.at[pl.ds(0, 1)], s5, r5, d=1).wait_recv()

    row = rows_b[0]

    sumsq = jnp.sum(jnp.where(lane1 == LANES - 1, row, 0.0), axis=1, keepdims=True)
    scores = jnp.where(lane1 < NDOM, row, 0.0)
    meansq = sumsq / (RANK * FF) + 1e-06
    ratio = scores / (RANK * FF * meansq)
    raised = weights * jnp.exp(step_rate * ratio)
    log_new = jnp.log(weights) + step_rate * ratio - jnp.log(jnp.sum(raised, axis=1, keepdims=True))
    log_ref[...] = log_new[:, 0:NDOM]
    new = jnp.where(lane1 < NDOM, jnp.exp(log_new), 0.0)
    update = combine(per_sequence(new), rank_rows)
    root = jnp.sqrt(meansq)
    for r in range(RANK):
        moved = learn_rate * update[r] / root
        out_ref[r : r + 1, :] = ada[r : r + 1, :] - moved[:, 0:COLS]

    @pl.when(scorer)
    def _():
        done(rows_a.at[pl.ds(0, 2 * SLAB)], s4, r4, d=1).wait_send()

        @pl.when(z < EARLY)
        def _():
            done(rows_a.at[pl.ds(0, 2 * SLAB - 1)], s4, r4, d=1).wait_send()

        @pl.when(z >= EARLY)
        def _():
            done(rows_a.at[pl.ds(0, 2 * SLAB)], s4, r4, d=1).wait_send()

        sent = got.at[pl.ds(1, BLOCKS - 1), pl.ds(0, len(SCORERS) * 2 - 1)]
        done(sent, s6, r6, d=1).wait_send()

    @pl.when(jnp.logical_not(scorer))
    def _():
        sent = got.at[pl.ds(1, BLOCKS - 1), pl.ds(0, len(SCORERS) * 2)]
        done(sent, s6, r6, d=1).wait_send()

    @pl.when(z == 0)
    def _():
        done(rows_a.at[pl.ds(0, N_Z - EARLY)], s5, r5, d=1).wait_send()

    done(part.at[pl.ds(1, N_MP - 1)], s1, r1, m=1).wait_send()
    done(seqbuf, s2, r2, s=1).wait_send()
    done(got.at[0, pl.ds(0, N_DP - 1)], s3, r3, d=1).wait_send()


def tail(moved, log_new, out_ref, log_ref):
    out_ref[...] = moved[...]
    log_ref[...] = log_new[...]


def body(hidden, cotangent, frozen_down, adapter, prior, domain_of):
    f32 = jnp.float32
    sem = pltpu.SemaphoreType.DMA
    out, log_new = pl.pallas_call(
        kernel,
        out_shape=(
            jax.ShapeDtypeStruct((RANK, COLS), f32),
            jax.ShapeDtypeStruct((1, NDOM), f32),
        ),
        in_specs=[pl.BlockSpec(memory_space=pl.ANY)] * 6,
        out_specs=(pl.BlockSpec(memory_space=pltpu.VMEM),) * 2,
        scratch_shapes=[
            pltpu.VMEM((ROWS, DM), jnp.bfloat16),
            pltpu.VMEM((ROWS, FFM), jnp.bfloat16),
            pltpu.VMEM((RANK, DM), jnp.bfloat16),
            pltpu.VMEM((RANK, COLS), f32),
            pltpu.VMEM((1, NDOM), f32),
            pltpu.SMEM((2,), jnp.int32),
            pltpu.VMEM((1, LANES), f32),
            pltpu.VMEM((N_MP, RANK, ROWS), f32),
            pltpu.VMEM((16, ROWS), f32),
            pltpu.VMEM((16, FFM), f32),
            pltpu.VMEM((N_SEQ, N_DP, RANK, LANES), SEND),
            pltpu.VMEM((N_SEQ - 1, N_DP, RANK, LANES), SEND),
            pltpu.VMEM((N_DP, RANK, LANES), SEND),
            pltpu.VMEM((BLOCKS, N_DP, RANK, LANES), SEND),
            pltpu.VMEM((BLOCKS, N_DP, RANK, LANES), f32),
            pltpu.VMEM((2 * SIDE * SLAB, 1, LANES), f32),
            pltpu.VMEM((1, 1, LANES), f32),
            sem((2,)),
            sem((CHUNKS,)),
            sem((3,)),
        ]
        + [sem] * 12
        + [pltpu.SemaphoreType.REGULAR((N_Z,))],
        compiler_params=pltpu.CompilerParams(
            collective_id=0, has_side_effects=True, vmem_limit_bytes=60 << 20
        ),
    )(hidden, cotangent, frozen_down.T, adapter.reshape(RANK, COLS), prior.reshape(1, NDOM), domain_of)
    out, log_new = pl.pallas_call(
        tail,
        out_shape=(
            jax.ShapeDtypeStruct((RANK, COLS), f32),
            jax.ShapeDtypeStruct((1, NDOM), f32),
        ),
        in_specs=[pl.BlockSpec(memory_space=pltpu.VMEM)] * 2,
        out_specs=(pl.BlockSpec(memory_space=pltpu.VMEM),) * 2,
    )(out, log_new)
    return out.reshape(1, RANK, COLS), log_new.reshape(NDOM)


def solution(mesh):
    return jax.shard_map(
        body,
        mesh=mesh,
        in_specs=(
            P(("dp", "seq"), "mp"),
            P(("dp", "seq"), "mp"),
            P("mp", None),
            P("mp", None, ("dp", "seq")),
            P(),
            P("dp"),
        ),
        out_specs=(P("mp", None, ("dp", "seq")), P()),
        check_vma=False,
    )
```

```python
import functools

import jax
import jax.numpy as jnp
from jax import lax
from jax.experimental import pallas as pl
from jax.experimental.pallas import tpu as pltpu
from jax.sharding import PartitionSpec as P

FF = 17920
NDOM = 48
RANK = 4
ROWS = 256
PIECE = 128
DM = 1664
FFM = 4480
N_DP = 32
N_SEQ = 4
N_MP = 4
COLS = FFM // (N_DP * N_SEQ)
LANES = 128
HALF = 64
CHUNKS = 2
SPAN = N_DP // CHUNKS
EDGES = tuple(min(c * 2304, FFM) for c in range(CHUNKS + 1))

SEND = jnp.bfloat16
N_Z = 16
SIDE = 2
EARLY = 3
SLAB = 32
BLOCKS = N_Z // (2 * SIDE)
SCORERS = (0, 1, 15, 14)
ORDER = (0, 1, 2, 3, 4, 5, 6, 7, 15, 8, 14, 9, 13, 10, 12, 11)
MESH = pl.DeviceIdType.MESH
step_rate = 1.0
learn_rate = 0.5


def kernel(
    hid_hbm, cot_hbm, fro_hbm, ada_hbm, pri_hbm, dom_hbm,
    out_ref, log_ref,
    hid, cot, fro, ada, pri, dom, wrow, part, lhs, g, spread, seqbuf, total, got, gotf, rows_a, rows_b,
    in_sem, cot_sem, small_sem, s1, r1, s2, r2, s3, r3, s4, r4, s5, r5, s6, r6, ready,
):
    dp, seq, mp = lax.axis_index("dp"), lax.axis_index("seq"), lax.axis_index("mp")

    def to(d=0, s=0, m=0):
        return {
            "dp": lax.rem(dp + d, N_DP),
            "seq": lax.rem(seq + s, N_SEQ),
            "mp": lax.rem(mp + m, N_MP),
        }

    z = lax.rem(dp, N_Z)
    place = jnp.where(z < 8, z, jnp.where(z < 12, 2 * z - 7, 38 - 2 * z))

    scorer = (z < SIDE) | (z >= N_Z - SIDE)
    stride = jnp.where(z < SIDE, SIDE, -SIDE)

    def at(d):
        return {"dp": d, "seq": seq, "mp": mp}

    def send(src, dst, ssem, rsem, target=None, **where):
        copy = pltpu.make_async_remote_copy(
            src_ref=src, dst_ref=dst, send_sem=ssem, recv_sem=rsem,
            device_id=to(**where) if target is None else target, device_id_type=MESH,
        )
        copy.start()

    def done(ref, ssem, rsem, **where):
        return pltpu.make_async_remote_copy(
            src_ref=ref, dst_ref=ref, send_sem=ssem, recv_sem=rsem,
            device_id=to(**where), device_id_type=MESH,
        )

    loads = [
        pltpu.make_async_copy(fro_hbm, fro, in_sem.at[0]),
        pltpu.make_async_copy(hid_hbm, hid, in_sem.at[1]),
    ]
    for load in loads:
        load.start()
    barrier = pltpu.get_barrier_semaphore()
    plane = [(s, m) for s in (2, 1, 3, 0) for m in (2, 3, 1, 0) if (s, m) != (0, 0)]
    near = [(0, m) for m in range(1, N_MP)] + [(s, 0) for s in range(1, N_SEQ)]
    for s, m in near:
        pl.semaphore_signal(barrier, inc=1, device_id=to(s=s, m=m), device_id_type=MESH)
    pl.semaphore_signal(barrier, inc=1, device_id=to(d=N_Z), device_id_type=MESH)
    for position, plane_z in enumerate(ORDER):

        @pl.when(place < position)
        def _():
            for x in range(2):
                pl.semaphore_signal(barrier, inc=1, device_id=at(x * N_Z + plane_z), device_id_type=MESH)


    lhs[...] = jnp.zeros_like(lhs)
    wrow[...] = jnp.zeros_like(wrow)

    for load in loads:
        load.wait()
    cot_loads = []
    for c in range(CHUNKS):
        cut = pl.ds(EDGES[c], EDGES[c + 1] - EDGES[c])
        load = pltpu.make_async_copy(cot_hbm.at[:, cut], cot.at[:, cut], cot_sem.at[c])
        load.start()
        cot_loads.append(load)
    small = [
        pltpu.make_async_copy(ada_hbm, ada, small_sem.at[0]),
        pltpu.make_async_copy(pri_hbm, pri, small_sem.at[1]),
        pltpu.make_async_copy(dom_hbm, dom, small_sem.at[2]),
    ]
    for load in small:
        load.start()

    partial = lax.dot_general(
        fro[...], hid[...], (((1,), (1,)), ((), ())), preferred_element_type=jnp.float32
    )
    part[0] = partial.astype(jnp.bfloat16).astype(jnp.float32)

    pl.semaphore_wait(barrier, len(near) + 1 + 2 * place)
    for position, plane_z in enumerate(ORDER):

        @pl.when(place > position)
        def _():
            for x in range(2):
                pl.semaphore_signal(
                    ready.at[z], inc=1, device_id=at(x * N_Z + plane_z), device_id_type=MESH
                )

    for m in range(1, N_MP):
        send(part.at[0], part.at[m], s1, r1, m=m)
    done(part.at[pl.ds(1, N_MP - 1)], s1, r1, m=1).wait_recv()
    down = part[0] + part[1] + part[2] + part[3]
    token = lax.broadcasted_iota(jnp.int32, (RANK, ROWS), 1)
    lhs[0:RANK] = jnp.where(token < PIECE, down, 0.0)
    lhs[8 : 8 + RANK] = jnp.where(token < PIECE, 0.0, down)
    left = lhs[...].astype(jnp.bfloat16)
    lane = lax.broadcasted_iota(jnp.int32, (8, LANES), 1)
    for c in range(CHUNKS):
        cut = slice(EDGES[c], EDGES[c + 1])
        cot_loads[c].wait()
        g[:, cut] = jnp.dot(left, cot[:, cut], preferred_element_type=jnp.float32)
        for p in range(c * SPAN * N_SEQ, (c + 1) * SPAN * N_SEQ):
            v, o = divmod(p * COLS, LANES)
            a = g[0:8, v * LANES : (v + 1) * LANES]
            b = g[8:16, v * LANES : (v + 1) * LANES]
            a = a if o == 0 else pltpu.roll(a, LANES - o, 1)
            b = pltpu.roll(b, (HALF - o) % LANES, 1) if o != HALF else b
            if o + COLS > LANES:
                a2 = g[0:8, (v + 1) * LANES : (v + 2) * LANES]
                b2 = g[8:16, (v + 1) * LANES : (v + 2) * LANES]
                a2 = pltpu.roll(a2, LANES - o, 1)
                b2 = pltpu.roll(b2, (HALF - o) % LANES, 1) if o != HALF else b2
                a = jnp.where(lane < LANES - o, a, a2)
                b = jnp.where(lane < HALF + LANES - o, b, b2)
            joined = jnp.where(lane < HALF, a, b)
            spread[p % N_SEQ, p // N_SEQ] = joined[0:RANK].astype(SEND)
        part_of = pl.ds(c * SPAN, SPAN)
        for s in (2, 1, 3):
            send(spread.at[lax.rem(seq + s, N_SEQ), part_of], seqbuf.at[s - 1, part_of], s2, r2, s=s)

    for load in small:
        load.wait()
    d0 = dom[0].astype(jnp.float32)
    d1 = dom[1].astype(jnp.float32)
    done(seqbuf, s2, r2, s=1).wait_recv()
    f32 = jnp.float32
    summed = (
        spread[seq].astype(f32) + seqbuf[0].astype(f32) + seqbuf[1].astype(f32) + seqbuf[2].astype(f32)
    )
    lane3 = lax.broadcasted_iota(jnp.int32, (N_DP, RANK, LANES), 2)
    summed = jnp.where(lane3 == COLS, d0, jnp.where(lane3 == HALF + COLS, d1, summed))
    total[...] = summed.astype(SEND)

    def exchange(plane_z, scored):
        position = ORDER.index(plane_z)

        @pl.when(place < position)
        def _():
            pl.semaphore_wait(ready.at[plane_z], 2)

        @pl.when(place != position)
        def _():
            for x in range(2):
                d = x * N_Z + plane_z
                if scored:
                    step = SIDE if plane_z < SIDE else -SIDE
                    for k in range(1, BLOCKS):
                        send(total.at[d + k * step], got.at[k, dp], s6, r6, target=at(d))
                send(total.at[d], got.at[0, dp], s3, r3, target=at(d))

    base = dp - z
    partner = lax.rem(dp + N_Z, N_DP)
    for plane_z in SCORERS:
        exchange(plane_z, True)

    @pl.when(scorer)
    def _():
        for k in range(1, BLOCKS):
            send(total.at[partner + k * stride], got.at[k, dp], s6, r6, target=at(partner))
            got[k, dp] = total[dp + k * stride]

    send(total.at[partner], got.at[0, dp], s3, r3, target=at(partner))
    got[0, dp] = total[dp]
    def rest():
        for plane_z in ORDER:
            if plane_z not in SCORERS:
                exchange(plane_z, False)

    pl.when(jnp.logical_not(scorer))(rest)
    wrow[:, 0:NDOM] = pri[...]
    prior = wrow[...]
    weights = prior / jnp.sum(prior, axis=1, keepdims=True)
    lane1 = lax.broadcasted_iota(jnp.int32, (1, LANES), 1)
    lane2 = lax.broadcasted_iota(jnp.int32, (N_DP, LANES), 1)
    low = lane2 < HALF

    done(got.at[0, pl.ds(0, N_DP - 1)], s3, r3, d=1).wait_recv()
    gotf[0] = got[0].astype(f32)
    rank_rows = [gotf[0, :, r, :] for r in range(RANK)]
    dom0 = rank_rows[0][:, COLS : COLS + 1]
    dom1 = rank_rows[0][:, HALF + COLS : HALF + COLS + 1]
    lanef = lane2.astype(f32)
    hot0 = (lanef == dom0).astype(f32)
    hot1 = (lanef == dom1).astype(f32)

    def per_sequence(row):
        return jnp.where(
            low,
            jnp.sum(hot0 * row, axis=1, keepdims=True),
            jnp.sum(hot1 * row, axis=1, keepdims=True),
        )

    def combine(scale, block):
        sums = [jnp.sum(scale * x, axis=0, keepdims=True) for x in block]
        return [x + pltpu.roll(x, HALF, 1) for x in sums]

    @pl.when(scorer)
    def _():
        others = got.at[pl.ds(1, BLOCKS - 1), pl.ds(0, N_DP - 1)]
        done(others, s6, r6, d=1).wait_recv()
        blocks = [rank_rows]
        for k in range(1, BLOCKS):
            gotf[k] = got[k].astype(f32)
            blocks.append([gotf[k, :, r, :] for r in range(RANK)])
        valid = (lane1 < COLS) | ((lane1 >= HALF) & (lane1 < HALF + COLS))
        mine_w = per_sequence(weights)
        square = jnp.zeros((1, LANES), f32)
        product = jnp.zeros((N_DP, LANES), f32)
        for block in blocks:
            mixture = [jnp.where(valid, x, 0.0) for x in combine(mine_w, block)]
            square += sum(x * x for x in mixture)
            product += sum(x * y for x, y in zip(block, mixture))
        sumsq = jnp.sum(jnp.where(lane1 < HALF, square, 0.0), axis=1, keepdims=True)
        score0 = jnp.sum(jnp.where(low, product, 0.0), axis=1, keepdims=True)
        score1 = jnp.sum(jnp.where(low, 0.0, product), axis=1, keepdims=True)
        row = jnp.sum(hot0 * score0 + hot1 * score1, axis=0, keepdims=True)
        row = jnp.where(lane1 == LANES - 1, sumsq, row)
        slot = jnp.where(z < SIDE, z, z - (N_Z - 2 * SIDE))
        mine = ((slot * 2 + dp // N_Z) * N_SEQ + seq) * N_MP + mp
        rows_a[mine] = row
        slab = [(d, s, m) for s in (2, 1, 3, 0) for d in (1, 0) for m in (2, 3, 1, 0)]

        @pl.loop(0, EARLY)
        def _(plane_z):
            for d, s, m in slab:
                target = {
                    "dp": lax.rem(dp // N_Z + d, 2) * N_Z + plane_z,
                    "seq": lax.rem(seq + s, N_SEQ),
                    "mp": lax.rem(mp + m, N_MP),
                }

                def push(target=target):
                    send(rows_a.at[mine], rows_a.at[mine], s4, r4, target=target)

                if (d, s, m) == (0, 0, 0):
                    pl.when(z != plane_z)(push)
                else:
                    push()

        rest()

    rows_in = 2 * SIDE * SLAB

    @pl.when(z < EARLY)
    def _():
        @pl.when(scorer)
        def _():
            done(rows_a.at[pl.ds(0, rows_in - 1)], s4, r4, d=1).wait_recv()

        @pl.when(jnp.logical_not(scorer))
        def _():
            done(rows_a, s4, r4, d=1).wait_recv()

        rows_b[0] = jnp.sum(rows_a[...], axis=0)

        @pl.when(z == 0)
        def _():
            for plane_z in (3, 4, 8, 5, 7, 6, 9, 10, 11, 12, 13, 14, 15):
                send(rows_b.at[0], rows_b.at[0], s5, r5, target=at(base + plane_z))

    @pl.when(z >= EARLY)
    def _():
        done(rows_b.at[pl.ds(0, 1)], s5, r5, d=1).wait_recv()

    row = rows_b[0]

    sumsq = jnp.sum(jnp.where(lane1 == LANES - 1, row, 0.0), axis=1, keepdims=True)
    scores = jnp.where(lane1 < NDOM, row, 0.0)
    meansq = sumsq / (RANK * FF) + 1e-06
    ratio = scores / (RANK * FF * meansq)
    raised = weights * jnp.exp(step_rate * ratio)
    log_new = jnp.log(weights) + step_rate * ratio - jnp.log(jnp.sum(raised, axis=1, keepdims=True))
    log_ref[...] = log_new[:, 0:NDOM]
    new = jnp.where(lane1 < NDOM, jnp.exp(log_new), 0.0)
    update = combine(per_sequence(new), rank_rows)
    root = jnp.sqrt(meansq)
    for r in range(RANK):
        moved = learn_rate * update[r] / root
        out_ref[r : r + 1, :] = ada[r : r + 1, :] - moved[:, 0:COLS]

    @pl.when(scorer)
    def _():
        done(rows_a.at[pl.ds(0, SLAB)], s4, r4, d=1).wait_send()

        @pl.when(z < EARLY)
        def _():
            done(rows_a.at[pl.ds(0, 2 * SLAB - 1)], s4, r4, d=1).wait_send()

        @pl.when(z >= EARLY)
        def _():
            done(rows_a.at[pl.ds(0, 2 * SLAB)], s4, r4, d=1).wait_send()

        sent = got.at[pl.ds(1, BLOCKS - 1), pl.ds(0, len(SCORERS) * 2 - 1)]
        done(sent, s6, r6, d=1).wait_send()

    @pl.when(jnp.logical_not(scorer))
    def _():
        sent = got.at[pl.ds(1, BLOCKS - 1), pl.ds(0, len(SCORERS) * 2)]
        done(sent, s6, r6, d=1).wait_send()

    @pl.when(z == 0)
    def _():
        done(rows_a.at[pl.ds(0, N_Z - EARLY)], s5, r5, d=1).wait_send()

    done(part.at[pl.ds(1, N_MP - 1)], s1, r1, m=1).wait_send()
    done(seqbuf, s2, r2, s=1).wait_send()
    done(got.at[0, pl.ds(0, N_DP - 1)], s3, r3, d=1).wait_send()


def tail(moved, log_new, out_ref, log_ref):
    out_ref[...] = moved[...]
    log_ref[...] = log_new[...]


def body(hidden, cotangent, frozen_down, adapter, prior, domain_of):
    f32 = jnp.float32
    sem = pltpu.SemaphoreType.DMA
    out, log_new = pl.pallas_call(
        kernel,
        out_shape=(
            jax.ShapeDtypeStruct((RANK, COLS), f32),
            jax.ShapeDtypeStruct((1, NDOM), f32),
        ),
        in_specs=[pl.BlockSpec(memory_space=pl.ANY)] * 6,
        out_specs=(pl.BlockSpec(memory_space=pltpu.VMEM),) * 2,
        scratch_shapes=[
            pltpu.VMEM((ROWS, DM), jnp.bfloat16),
            pltpu.VMEM((ROWS, FFM), jnp.bfloat16),
            pltpu.VMEM((RANK, DM), jnp.bfloat16),
            pltpu.VMEM((RANK, COLS), f32),
            pltpu.VMEM((1, NDOM), f32),
            pltpu.SMEM((2,), jnp.int32),
            pltpu.VMEM((1, LANES), f32),
            pltpu.VMEM((N_MP, RANK, ROWS), f32),
            pltpu.VMEM((16, ROWS), f32),
            pltpu.VMEM((16, FFM), f32),
            pltpu.VMEM((N_SEQ, N_DP, RANK, LANES), SEND),
            pltpu.VMEM((N_SEQ - 1, N_DP, RANK, LANES), SEND),
            pltpu.VMEM((N_DP, RANK, LANES), SEND),
            pltpu.VMEM((BLOCKS, N_DP, RANK, LANES), SEND),
            pltpu.VMEM((BLOCKS, N_DP, RANK, LANES), f32),
            pltpu.VMEM((2 * SIDE * SLAB, 1, LANES), f32),
            pltpu.VMEM((1, 1, LANES), f32),
            sem((2,)),
            sem((CHUNKS,)),
            sem((3,)),
        ]
        + [sem] * 12
        + [pltpu.SemaphoreType.REGULAR((N_Z,))],
        compiler_params=pltpu.CompilerParams(
            collective_id=0, has_side_effects=True, vmem_limit_bytes=60 << 20
        ),
    )(hidden, cotangent, frozen_down.T, adapter.reshape(RANK, COLS), prior.reshape(1, NDOM), domain_of)
    out, log_new = pl.pallas_call(
        tail,
        out_shape=(
            jax.ShapeDtypeStruct((RANK, COLS), f32),
            jax.ShapeDtypeStruct((1, NDOM), f32),
        ),
        in_specs=[pl.BlockSpec(memory_space=pltpu.VMEM)] * 2,
        out_specs=(pl.BlockSpec(memory_space=pltpu.VMEM),) * 2,
    )(out, log_new)
    return out.reshape(1, RANK, COLS), log_new.reshape(NDOM)


def solution(mesh):
    return jax.shard_map(
        body,
        mesh=mesh,
        in_specs=(
            P(("dp", "seq"), "mp"),
            P(("dp", "seq"), "mp"),
            P("mp", None),
            P("mp", None, ("dp", "seq")),
            P(),
            P("dp"),
        ),
        out_specs=(P("mp", None, ("dp", "seq")), P()),
        check_vma=False,
    )
```
